512 devices in a mesh: seq: 16 (over z, core), head: 32 (over x, y).
Axes of the slice: x: 4, y: 8, z: 8, core: 2. Of those that a mesh axis runs over, the one named last changes fastest.
Arguments:
- values: bfloat16 [16384, 8192], P('seq', 'head'), may hold values from -6 to 6
- gate_z: bfloat16 [16384, 8192], P('seq', 'head'), may hold values from -6 to 6
- b_keys: bfloat16 [16384, 8, 128], P('seq'), may hold values from -0.5 to 0.5
- c_queries: bfloat16 [16384, 8, 128], P('seq'), may hold values from -6 to 6
- log_decay: float32 [16384, 128], P('seq', 'head'), may hold values from -2.5 to 0
- level_weight: float32 [16384, 128, 9], P('seq', 'head'), may hold values from 0.2 to 2
- doc_start: int32 [256], replicated, may hold values 0 or 1
- norm_gain: float32 [8192], replicated, may hold values from 0.25 to 1.75
Outputs:
- normed: bfloat16 [16384, 8192], P(('seq', 'head'))
The draws below stay inside these ranges and needn't reach their ends.
All inputs are finite; a program needn't handle non-finite values.
Results may differ from the reference program's by a relative error of at most 0.0049.
Values may be sent and summed in bfloat16 or wider, within the bound.
A program may use at most 64 MiB of HBM per device.

```python
import math
import jax
import jax.numpy as jnp
from jax import lax

MIXER_HEADS = 128
HEAD_DIM = 64
STATE = 128
GROUPS = 8
SPAN = 64
WINDOW_TOKENS = 16384
SPANS = 256
LEVELS = 9


def draw_log_decay(key, part):
    complete_keys = jax.random.split(key, 7)
    fast_share = 0.5
    fast_heads = jax.random.uniform(complete_keys[0], (MIXER_HEADS,)) < fast_share
    fast_rate = jnp.exp(jax.random.uniform(complete_keys[1], (MIXER_HEADS,), minval=math.log(1.0 / 50.0), maxval=math.log(1.0 / 30.0)))
    slow_rate = 0.3 * math.log(10.0) / WINDOW_TOKENS * jnp.exp(jax.random.uniform(complete_keys[2], (MIXER_HEADS,), minval=-0.3, maxval=0.3))
    default_rate = jnp.where(fast_heads, fast_rate, slow_rate)
    block_multiplier = jnp.exp(jax.random.uniform(complete_keys[3], (WINDOW_TOKENS // SPAN, 1, MIXER_HEADS), minval=-math.log(2.0), maxval=math.log(2.0)))
    block_multiplier = jnp.broadcast_to(block_multiplier, (WINDOW_TOKENS // SPAN, SPAN, MIXER_HEADS)).reshape(WINDOW_TOKENS, MIXER_HEADS)
    token_multiplier = jax.random.uniform(complete_keys[4], (WINDOW_TOKENS, MIXER_HEADS), minval=0.5, maxval=1.5)
    surge_position = jax.random.randint(complete_keys[5], (3,), 0, WINDOW_TOKENS)
    surge_length = jax.random.uniform(complete_keys[6], (3, MIXER_HEADS), minval=0.22, maxval=0.69)
    token_positions = jnp.arange(WINDOW_TOKENS)
    match_count = (token_positions[:, None] == surge_position[None, :]).astype(jnp.float32)
    surge_list = jnp.dot(match_count, surge_length)
    return (-(default_rate[None, :] * block_multiplier * token_multiplier) - surge_list).astype(jnp.float32)


def place_ends(array, key, low, top_value):
    spot = [jax.random.randint(jax.random.fold_in(key, axis), (), 0, length) for axis, length in enumerate(array.shape)]
    widest = array.shape.index(max(array.shape))
    beside = spot[:widest] + [(spot[widest] + 1) % array.shape[widest]] + spot[widest + 1:]
    return array.at[tuple(spot)].set(low).at[tuple(beside)].set(top_value)


def levels(own_key, shape, shards, smallest, largest):
    level, own = 1.0, jax.random.fold_in(own_key, 6)
    for position, parts in shards:
        draws = jnp.exp(jax.random.uniform(jax.random.fold_in(own, position), (parts,), jnp.float32, smallest / len(shards), largest / len(shards)))
        level = level * jnp.repeat(draws, shape[position] // parts).reshape([-1 if axis == position else 1 for axis in range(len(shape))])
    return level


def bell_draw(rng, dims, scale, limit, cuts=(), kind=jnp.bfloat16):
    values = jax.random.normal(rng, dims, jnp.float32) * scale
    if len(cuts) > 0:
        values = levels(rng, dims, cuts, -0.22, 0.18) * values
    return jnp.clip(values, min=-limit, max=limit).astype(kind)


def setup_inputs(seed: int = 0) -> dict:
    key_of = jax.random.split(jax.random.key(seed), 9)
    return {
        "values": bell_draw(key_of[0], (WINDOW_TOKENS, MIXER_HEADS * HEAD_DIM), 1.0, 6.0, ((0, 16), (1, 32))),
        "gate_z": bell_draw(key_of[1], (WINDOW_TOKENS, MIXER_HEADS * HEAD_DIM), 1.0, 6.0, ((0, 16), (1, 32))),
        "b_keys": bell_draw(key_of[2], (WINDOW_TOKENS, GROUPS, STATE), STATE ** -0.5, 0.5, ((0, 16),)),
        "c_queries": bell_draw(key_of[3], (WINDOW_TOKENS, GROUPS, STATE), 1.0, 6.0, ((0, 16),)),
        "log_decay": draw_log_decay(jax.random.fold_in(key_of[8], 71), 0),
        "level_weight": jnp.clip(jnp.exp(math.log(2.0) - 2.3025851 * jax.random.uniform(key_of[5], (WINDOW_TOKENS, MIXER_HEADS, LEVELS), jnp.float32) ** levels(key_of[5], (WINDOW_TOKENS, MIXER_HEADS, LEVELS), ((0, 16), (1, 32)), -0.2, 0.2)), 0.2, 2.0),
        "doc_start": place_ends((jax.random.randint(key_of[6], (SPANS,), 0, SPANS) < 2).astype(jnp.int32), jax.random.fold_in(key_of[6], 1), 0, 1),
        "norm_gain": jnp.clip(1.0 + 0.15 * jax.random.normal(key_of[7], (MIXER_HEADS * HEAD_DIM,), jnp.float32), 0.25, 1.75),
    }


def bit_count(operand, bit_width):
    result = jnp.zeros_like(operand)
    for offset in range(bit_width):
        result = result + (jnp.right_shift(operand, offset) > 0).astype(jnp.int32)
    return result

def reference(values, gate_z, b_keys, c_queries, log_decay, level_weight, doc_start, norm_gain):
    per_group = MIXER_HEADS // GROUPS
    highest = lax.Precision.HIGHEST
    counts = jnp.cumsum(doc_start).astype(jnp.int32)
    span_index = jnp.arange(SPANS, dtype=jnp.int32)
    span_level = bit_count(jnp.bitwise_xor(span_index[:, None], span_index[None, :]), LEVELS - 1)
    earlier = (span_index[None, :] < span_index[:, None]) & (counts[:, None] == counts[None, :])
    within = jnp.tril(jnp.ones((SPAN, SPAN), dtype=bool))
    level_masks = jnp.stack([span_level == level_index for level_index in range(1, LEVELS)]).astype(jnp.float32)

    def one_head(head_index):
        group_index = head_index // per_group
        key_rows = lax.dynamic_index_in_dim(b_keys, group_index, 1, keepdims=False).astype(jnp.float32).reshape(SPANS, SPAN, STATE)
        query_rows = lax.dynamic_index_in_dim(c_queries, group_index, 1, keepdims=False).astype(jnp.float32).reshape(SPANS, SPAN, STATE)
        inputs = lax.dynamic_slice_in_dim(values, head_index * HEAD_DIM, HEAD_DIM, 1).astype(jnp.float32).reshape(SPANS, SPAN, HEAD_DIM)
        decay_step = lax.dynamic_index_in_dim(log_decay, head_index, 1, keepdims=False)
        weights = lax.dynamic_index_in_dim(level_weight, head_index, 1, keepdims=False).reshape(SPANS, SPAN, LEVELS)
        decay_sum = jnp.cumsum(decay_step).reshape(SPANS, SPAN)
        span_start = decay_sum[:, 0] - decay_step.reshape(SPANS, SPAN)[:, 0]
        span_end = decay_sum[:, SPAN - 1]
        scores = jnp.einsum('ctn,csn->cts', query_rows, key_rows, precision=highest)
        log_gap = jnp.where(within[None], decay_sum[:, :, None] - decay_sum[:, None, :], -jnp.inf)
        masked = scores * jnp.exp(log_gap) * weights[:, :, 0][:, :, None]
        result = jnp.einsum('cts,csp->ctp', masked, inputs, precision=highest)
        key_scale = jnp.exp(span_end[:, None] - decay_sum)
        states = jnp.einsum('csn,csp->cnp', key_rows * key_scale[:, :, None], inputs, precision=highest)
        carry = jnp.exp(jnp.where(earlier, span_start[:, None] - span_end[None, :], -jnp.inf))
        incoming = jnp.einsum('lij,jnp->linp', level_masks * carry[None], states, precision=highest)
        projected = jnp.einsum('itn,linp->itlp', query_rows, incoming, precision=highest)
        far_coef = weights[:, :, 1:] * jnp.exp(decay_sum - span_start[:, None])[:, :, None]
        result = result + jnp.einsum('itl,itlp->itp', far_coef, projected, precision=highest)
        return result.reshape(WINDOW_TOKENS, HEAD_DIM)
    mixer = lax.map(one_head, jnp.arange(MIXER_HEADS, dtype=jnp.int32))
    mixer = jnp.transpose(mixer, (1, 0, 2)).reshape(WINDOW_TOKENS, MIXER_HEADS * HEAD_DIM).astype(jnp.bfloat16)
    gated = mixer.astype(jnp.float32) * jax.nn.silu(gate_z.astype(jnp.float32))
    grouped = gated.reshape(WINDOW_TOKENS, GROUPS, MIXER_HEADS * HEAD_DIM // GROUPS)
    inverse_rms = lax.rsqrt(lax.optimization_barrier(jnp.mean(grouped * grouped, axis=2, keepdims=True)) + 1e-05)
    return ((grouped * inverse_rms).reshape(WINDOW_TOKENS, MIXER_HEADS * HEAD_DIM) * norm_gain[None, :]).astype(jnp.bfloat16)
```

```python
import jax
import jax.numpy as jnp
from jax import lax
from jax.experimental import pallas as pl
from jax.experimental.pallas import tpu as pltpu
from jax.sharding import PartitionSpec as P

MESH = pl.DeviceIdType.MESH
F32 = jnp.float32
BF16 = jnp.bfloat16
CHUNK = 128
SPAN = 64
HEADS = 4
DIM = 64
STATE = 128
PER_GROUP = 16
RESET = 128.0


def dot(a, b):
    return jnp.dot(a, b, preferred_element_type=F32)


def kernel(
    n_seq, n_head, b_hbm, c_hbm, v_hbm, g_hbm, decay_hbm, level_hbm, gain_hbm, doc_ref, out_ref,
    pair, wide, keys, query_t, raw, value_t, gate, silu, decay, level, gain,
    ds, tot, key_w, query_w, near, acc, own_state, sib_state, own_decay, all_decay,
    chip_state, chip_states, coef, own_levels, sib_levels, levels, outgoing, arrived,
    load_sem, swap_sem, decay_send, decay_recv, chip_send, chip_recv, rows_send, rows_recv,
):
    me = lax.axis_index("head")
    seq = lax.axis_index("seq")
    z, core = seq // 2, lax.rem(seq, 2)
    n_z = n_seq // 2
    far_levels = n_z.bit_length()
    group = me * HEADS // PER_GROUP
    tokens = v_hbm.shape[0]
    chunks = tokens // CHUNK
    width = HEADS * DIM
    rows_out = tokens // n_head
    per_chunk = CHUNK // rows_out

    loads = [
        pltpu.make_async_copy(decay_hbm, decay, load_sem.at[0]),
        pltpu.make_async_copy(v_hbm, raw, load_sem.at[1]),
        pltpu.make_async_copy(b_hbm.at[:, group // 2], pair.at[0], load_sem.at[2]),
        pltpu.make_async_copy(c_hbm.at[:, group // 2], pair.at[1], load_sem.at[3]),
        pltpu.make_async_copy(level_hbm, level, load_sem.at[4]),
        pltpu.make_async_copy(g_hbm, gate, load_sem.at[5]),
        pltpu.make_async_copy(gain_hbm, gain, load_sem.at[6]),
    ]
    for load in loads:
        load.start()

    barrier = pltpu.get_barrier_semaphore()

    def greet_head(r, _):
        pl.semaphore_signal(
            barrier, inc=1, device_id={"head": lax.rem(me + r, n_head)}, device_id_type=MESH
        )
        return 0

    def greet_seq(r, _):
        pl.semaphore_signal(
            barrier, inc=1, device_id={"seq": lax.rem(seq + r, n_seq)}, device_id_type=MESH
        )
        return 0

    lax.fori_loop(1, n_seq, greet_seq, 0)
    lax.fori_loop(1, n_head, greet_head, 0)

    loads[0].wait()
    lane4 = lax.broadcasted_iota(jnp.int32, (HEADS, CHUNK), 1)
    pieces = []
    for i in range(chunks):
        piece = decay[:, i * CHUNK : (i + 1) * CHUNK]
        for half in range(2):
            begins = doc_ref[seq * (tokens // SPAN) + 2 * i + half] != 0
            drop = jnp.where(begins, RESET, 0.0)
            piece = piece - jnp.where(lane4 == half * SPAN, drop, 0.0)
        pieces.append(piece)
    run = jnp.concatenate(pieces, axis=0)
    lane = lax.broadcasted_iota(jnp.int32, run.shape, 1)
    shift = 1
    while shift < CHUNK:
        run = run + jnp.where(lane >= shift, pltpu.roll(run, shift, 1), 0.0)
        shift *= 2
    total = jnp.broadcast_to(run[:, CHUNK - 1 : CHUNK], run.shape)
    ds[...] = jnp.zeros_like(ds)
    before = jnp.zeros((HEADS, CHUNK), F32)
    after = jnp.zeros((HEADS, CHUNK), F32)
    for i in range(chunks):
        part = slice(i * HEADS, (i + 1) * HEADS)
        ds[i, 0:HEADS, :] = run[part]
        tot[i] = total[part]
        query_w[i] = jnp.exp(before + run[part])
        before = before + total[part]
    for i in reversed(range(chunks)):
        part = slice(i * HEADS, (i + 1) * HEADS)
        key_w[i] = jnp.exp(after + (total[part] - run[part]))
        after = after + total[part]
    own_decay[...] = jnp.zeros_like(own_decay)
    own_decay[0:HEADS, :] = before

    def scaled(i, weights):
        parts = [
            value_t[i, h * DIM : (h + 1) * DIM, :].astype(F32) * weights[h : h + 1, :]
            for h in range(HEADS)
        ]
        return jnp.concatenate(parts, axis=0).astype(BF16)

    def at(i):
        return pl.ds(pl.multiple_of(i * CHUNK, CHUNK), CHUNK)

    loads[2].wait()
    wide[...] = pair[0].reshape(2 * tokens, STATE).astype(F32)
    keys[...] = wide[pl.ds(lax.rem(group, 2), tokens, stride=2), :].astype(BF16)
    loads[1].wait()
    own_state[...] = jnp.zeros_like(own_state)

    def state_step(i, _):
        value_t[i] = raw[at(i), :].T
        own_state[...] += dot(scaled(i, key_w[i]), keys[at(i), :])
        return 0

    lax.fori_loop(0, chunks, state_step, 0)

    pl.semaphore_wait(barrier, n_seq - 1 + n_head - 1)

    swap = pltpu.make_async_remote_copy(
        src_ref=own_state, dst_ref=sib_state, send_sem=swap_sem.at[0], recv_sem=swap_sem.at[1],
        device_id={"seq": 2 * z + 1 - core}, device_id_type=MESH,
    )
    swap.start()

    def decay_copy(other, slot):
        return pltpu.make_async_remote_copy(
            src_ref=own_decay, dst_ref=all_decay.at[slot], send_sem=decay_send.at[other],
            recv_sem=decay_recv.at[slot], device_id={"seq": other}, device_id_type=MESH,
        )

    def send_decay(r, _):
        decay_copy(lax.rem(seq + r, n_seq), seq).start()
        return 0

    lax.fori_loop(1, n_seq, send_decay, 0)
    all_decay[pl.ds(seq, 1)] = own_decay[...][None]

    loads[3].wait()
    wide[...] = pair[1].reshape(2 * tokens, STATE).astype(F32)

    def turn_queries(i, _):
        start = lax.rem(group, 2) + i * (2 * CHUNK)
        query_t[i] = wide[pl.ds(start, CHUNK, stride=2), :].T.astype(BF16)
        return 0

    lax.fori_loop(0, chunks, turn_queries, 0)

    def wait_decay(r, _):
        other = lax.rem(seq + r, n_seq)
        decay_copy(other, other).wait_recv()
        return 0

    lax.fori_loop(1, n_seq, wait_decay, 0)
    swap.wait_recv()

    is_upper = core == 1
    half = width // 2
    mine = pl.ds(pl.multiple_of(core * half, half), half)
    theirs = pl.ds(pl.multiple_of((1 - core) * half, half), half)
    upper_decay = all_decay[2 * z + 1]
    through = jnp.exp(upper_decay)
    parts = []
    for j in range(2):
        rows = pl.ds(pl.multiple_of(core * half + j * DIM, DIM), DIM)
        fade = jnp.where(is_upper, through[2 + j : 3 + j, :], through[j : j + 1, :])
        here, there = own_state[rows, :], sib_state[rows, :]
        low = jnp.where(is_upper, there, here)
        high = jnp.where(is_upper, here, there)
        parts.append(low * fade + high)
    chip_state[...] = jnp.concatenate(parts, axis=0).astype(BF16)

    def chip_copy(other, slot):
        return pltpu.make_async_remote_copy(
            src_ref=chip_state, dst_ref=chip_states.at[slot], send_sem=chip_send.at[other],
            recv_sem=chip_recv.at[slot], device_id={"seq": 2 * other + core}, device_id_type=MESH,
        )

    def send_chip(r, _):
        chip_copy(lax.rem(z + r, n_z), z).start()
        return 0

    lax.fori_loop(1, n_z, send_chip, 0)

    gap = jnp.zeros((8, CHUNK), F32)
    for j in reversed(range(n_z)):
        coef[j] = jnp.where(j < z, jnp.exp(gap), 0.0)
        gap = gap + jnp.where(j < z, all_decay[2 * j] + all_decay[2 * j + 1], 0.0)
    levels[0] = jnp.where(is_upper, sib_state[...], 0.0).astype(BF16)

    loads[4].wait()
    loads[5].wait()
    acc[...] = jnp.zeros_like(acc)
    sub_i = lax.broadcasted_iota(jnp.int32, (CHUNK, CHUNK), 0)
    lane_i = lax.broadcasted_iota(jnp.int32, (CHUNK, CHUNK), 1)
    causal = sub_i <= lane_i
    early = sub_i < SPAN
    first_half = lax.broadcasted_iota(jnp.int32, (1, CHUNK), 1) < SPAN
    local_levels = acc.shape[0]

    def near_step(i, _):
        g = gate[at(i), :].astype(F32)
        silu[i] = g / (1.0 + jnp.exp(-g))
        turned = query_t[i]
        block = keys[at(i), :]
        scores = dot(block, turned)
        run_i = ds[i]
        columns = run_i.T
        weight = jnp.exp(run_i)
        tot_i = tot[i]
        into = dot(
            acc[...].reshape(local_levels * width, STATE).astype(BF16), turned
        ).reshape(local_levels, width, CHUNK)
        for h in range(HEADS):
            rows = slice(h * DIM, (h + 1) * DIM)
            fall = run_i[h : h + 1, :] - jnp.broadcast_to(columns[:, h : h + 1], (CHUNK, CHUNK))
            same = level[0, h : h + 1, at(i)]
            cross = jnp.where(first_half, same, level[1, h : h + 1, at(i)])
            mixed = jnp.exp(jnp.where(causal, fall, -1e30)) * jnp.where(early, cross, same) * scores
            result = dot(value_t[i, rows, :], mixed.astype(BF16))
            for k in range(local_levels):
                on = (lax.shift_right_logical(i, k) & 1).astype(F32)
                factor = level[2 + k, h : h + 1, at(i)] * weight[h : h + 1, :] * on
                result = result + into[k, rows, :] * factor
            near[i, rows, :] = result
        state = dot(scaled(i, jnp.exp(tot_i - run_i[0:HEADS])), block)
        keep = jnp.exp(tot_i)
        for k in range(local_levels):
            low = (1 - (lax.shift_right_logical(i, k) & 1)).astype(F32)
            held = (lax.rem(i, 2 ** (k + 1)) != 0).astype(F32)
            for h in range(HEADS):
                rows = slice(h * DIM, (h + 1) * DIM)
                acc[k, rows, :] = acc[k, rows, :] * (keep[h : h + 1, :] * held) + state[rows, :] * low
        return 0

    lax.fori_loop(0, chunks, near_step, 0)

    def wait_chip(r, _):
        other = lax.rem(z + r, n_z)
        chip_copy(other, other).wait_recv()
        return 0

    lax.fori_loop(1, n_z, wait_chip, 0)
    for k in range(far_levels - 1):
        first = (lax.shift_right_logical(z, k) ^ 1) * 2**k
        for j in range(2):
            total_j = jnp.zeros((DIM, STATE), F32)
            for n in range(2**k):
                row = coef[first + n]
                fade = jnp.where(is_upper, row[2 + j : 3 + j, :], row[j : j + 1, :])
                total_j = total_j + chip_states[first + n, j * DIM : (j + 1) * DIM, :].astype(F32) * fade
            own_levels[k, j * DIM : (j + 1) * DIM, :] = total_j.astype(BF16)
    share = pltpu.make_async_remote_copy(
        src_ref=own_levels, dst_ref=sib_levels, send_sem=swap_sem.at[2], recv_sem=swap_sem.at[3],
        device_id={"seq": 2 * z + 1 - core}, device_id_type=MESH,
    )
    share.start()
    for k in range(far_levels - 1):
        levels[1 + k, mine, :] = own_levels[k]
    share.wait_recv()
    for k in range(far_levels - 1):
        levels[1 + k, theirs, :] = sib_levels[k]

    def row_copy(target, source, i, k):
        return pltpu.make_async_remote_copy(
            src_ref=outgoing.at[i, pl.ds(pl.multiple_of(k * rows_out, rows_out), rows_out), :],
            dst_ref=arrived.at[:, pl.ds(pl.multiple_of(source * width, width), width)],
            send_sem=rows_send.at[target], recv_sem=rows_recv.at[source],
            device_id={"head": target}, device_id_type=MESH,
        )

    own_chunk = me // per_chunk
    base = level.shape[0] - far_levels

    def far_step(r, _):
        i = lax.rem(own_chunk + r, chunks)
        into = dot(
            levels[...].reshape(far_levels * width, STATE), query_t[i]
        ).reshape(far_levels, width, CHUNK)
        weight = query_w[i]
        further = weight * jnp.where(is_upper, jnp.exp(all_decay[2 * z])[0:HEADS], 1.0)
        columns = []
        for h in range(HEADS):
            rows = slice(h * DIM, (h + 1) * DIM)
            result = near[i, rows, :]
            for k in range(far_levels):
                from_start = weight if k == 0 else further
                factor = level[base + k, h : h + 1, at(i)] * from_start[h : h + 1, :]
                result = result + into[k, rows, :] * factor
            columns.append(result)
        mixed = jnp.concatenate(columns, axis=0).T
        outgoing[i] = (mixed * silu[i]).astype(BF16)
        for k in range(per_chunk):
            target = i * per_chunk + k

            @pl.when(target != me)
            def _():
                row_copy(target, me, i, k).start()

            @pl.when(target == me)
            def _():
                arrived[:, pl.ds(pl.multiple_of(me * width, width), width)] = outgoing[
                    i, k * rows_out : (k + 1) * rows_out, :
                ]

        return 0

    lax.fori_loop(0, chunks, far_step, 0)

    loads[6].wait()
    group_width = PER_GROUP * DIM
    per_group = group_width // width
    groups = n_head // per_group

    def norm_step(r, _):
        g = lax.rem(me // per_group - r + groups, groups)
        for k in range(per_group):
            source = g * per_group + k

            @pl.when(source != me)
            def _():
                row_copy(source, source, 0, 0).wait_recv()

        x = arrived[:, pl.ds(pl.multiple_of(g * group_width, group_width), group_width)].astype(F32)
        inverse = lax.rsqrt(jnp.sum(x * x, axis=1, keepdims=True) * (1.0 / group_width) + 1e-05)
        for k in range(group_width // CHUNK):
            y = x[:, k * CHUNK : (k + 1) * CHUNK] * inverse * gain[pl.ds(g * (group_width // CHUNK) + k, 1), :]
            out_ref[:, pl.ds(pl.multiple_of(g * group_width + k * CHUNK, CHUNK), CHUNK)] = y.astype(BF16)
        return 0

    lax.fori_loop(0, groups, norm_step, 0)

    def drain_rows(r, _):
        row_copy(lax.rem(me + r, n_head), me, 0, 0).wait_send()
        return 0

    lax.fori_loop(1, n_head, drain_rows, 0)

    def drain_decay(r, _):
        decay_copy(lax.rem(seq + r, n_seq), seq).wait_send()
        return 0

    lax.fori_loop(1, n_seq, drain_decay, 0)

    def drain_chip(r, _):
        chip_copy(lax.rem(z + r, n_z), z).wait_send()
        return 0

    lax.fori_loop(1, n_z, drain_chip, 0)
    swap.wait_send()
    share.wait_send()


def solution(mesh):
    n_seq, n_head = mesh.shape["seq"], mesh.shape["head"]
    n_z = n_seq // 2

    def body(values, gate_z, b_keys, c_queries, log_decay, level_weight, doc_start, norm_gain):
        tokens, width = values.shape
        chunks = tokens // CHUNK
        n_levels = level_weight.shape[2]
        far_levels = n_z.bit_length()
        local_levels = chunks.bit_length() - 1
        groups = b_keys.shape[1]
        any_space = pl.BlockSpec(memory_space=pl.ANY)
        rows = tokens // n_head
        dma = pltpu.SemaphoreType.DMA

        def run(*args):
            return kernel(n_seq, n_head, *args)

        return pl.pallas_call(
            run,
            out_shape=jax.ShapeDtypeStruct((rows, n_head * width), BF16),
            in_specs=[any_space] * 7 + [pl.BlockSpec(memory_space=pltpu.SMEM)],
            out_specs=pl.BlockSpec(memory_space=pltpu.VMEM),
            scratch_shapes=[
                pltpu.VMEM((2, tokens, 2, STATE), BF16),
                pltpu.VMEM((2 * tokens, STATE), F32),
                pltpu.VMEM((tokens, STATE), BF16),
                pltpu.VMEM((chunks, STATE, CHUNK), BF16),
                pltpu.VMEM((tokens, width), BF16),
                pltpu.VMEM((chunks, width, CHUNK), BF16),
                pltpu.VMEM((tokens, width), BF16),
                pltpu.VMEM((chunks, CHUNK, width), F32),
                pltpu.VMEM((HEADS, tokens), F32),
                pltpu.VMEM((n_levels, HEADS, tokens), F32),
                pltpu.VMEM((n_head * width // CHUNK, CHUNK), F32),
                pltpu.VMEM((chunks, 8, CHUNK), F32),
                pltpu.VMEM((chunks, HEADS, CHUNK), F32),
                pltpu.VMEM((chunks, HEADS, CHUNK), F32),
                pltpu.VMEM((chunks, HEADS, CHUNK), F32),
                pltpu.VMEM((chunks, width, CHUNK), F32),
                pltpu.VMEM((local_levels, width, STATE), F32),
                pltpu.VMEM((width, STATE), F32),
                pltpu.VMEM((width, STATE), F32),
                pltpu.VMEM((8, CHUNK), F32),
                pltpu.VMEM((n_seq, 8, CHUNK), F32),
                pltpu.VMEM((width // 2, STATE), BF16),
                pltpu.VMEM((n_z, width // 2, STATE), BF16),
                pltpu.VMEM((n_z, 8, CHUNK), F32),
                pltpu.VMEM((far_levels - 1, width // 2, STATE), BF16),
                pltpu.VMEM((far_levels - 1, width // 2, STATE), BF16),
                pltpu.VMEM((far_levels, width, STATE), BF16),
                pltpu.VMEM((chunks, CHUNK, width), BF16),
                pltpu.VMEM((rows, n_head * width), BF16),
                dma((7,)),
                dma((4,)),
                dma((n_seq,)),
                dma((n_seq,)),
                dma((n_z,)),
                dma((n_z,)),
                dma((n_head,)),
                dma((n_head,)),
            ],
            compiler_params=pltpu.CompilerParams(collective_id=0, has_side_effects=True),
        )(
            b_keys.reshape(tokens, groups // 2, 2, STATE),
            c_queries.reshape(tokens, groups // 2, 2, STATE),
            values,
            gate_z,
            log_decay.T,
            level_weight.transpose(2, 1, 0),
            norm_gain.reshape(n_head * width // CHUNK, CHUNK),
            doc_start,
        )

    in_specs = (
        P("seq", "head"),
        P("seq", "head"),
        P("seq", None, None),
        P("seq", None, None),
        P("seq", "head"),
        P("seq", "head", None),
        P(),
        P(),
    )
    out_specs = P(("seq", "head"), None)
    return jax.shard_map(body, mesh=mesh, in_specs=in_specs, out_specs=out_specs, check_vma=False)
```

```python
import jax
import jax.numpy as jnp
from jax import lax
from jax.experimental import pallas as pl
from jax.experimental.pallas import tpu as pltpu
from jax.sharding import PartitionSpec as P

MESH = pl.DeviceIdType.MESH
F32 = jnp.float32
BF16 = jnp.bfloat16
CHUNK = 128
SPAN = 64
HEADS = 4
DIM = 64
STATE = 128
PER_GROUP = 16
PAIRS = HEADS // 2
RESET = 128.0


def dot(a, b):
    return jnp.dot(a, b, preferred_element_type=F32)


def kernel(
    n_seq, n_head, b_hbm, c_hbm, v_hbm, g_hbm, decay_hbm, level_hbm, gain_hbm, doc_ref, out_ref,
    pair, wide, keys, query_t, raw, value_t, gate, silu, decay, level, gain,
    ds, tot, key_w, query_w, near, acc, own_state, sib_state, own_decay, all_decay,
    chip_state, chip_states, coef, own_levels, sib_levels, levels, outgoing, arrived,
    load_sem, swap_sem, decay_send, decay_recv, chip_send, chip_recv, rows_send, rows_recv,
):
    me = lax.axis_index("head")
    seq = lax.axis_index("seq")
    z, core = seq // 2, lax.rem(seq, 2)
    n_z = n_seq // 2
    far_levels = n_z.bit_length()
    group = me * HEADS // PER_GROUP
    tokens = v_hbm.shape[0]
    chunks = tokens // CHUNK
    width = HEADS * DIM
    rows_out = tokens // n_head

    loads = [
        pltpu.make_async_copy(decay_hbm, decay, load_sem.at[0]),
        pltpu.make_async_copy(v_hbm, raw, load_sem.at[1]),
        pltpu.make_async_copy(b_hbm.at[:, group // 2], pair.at[0], load_sem.at[2]),
        pltpu.make_async_copy(c_hbm.at[:, group // 2], pair.at[1], load_sem.at[3]),
        pltpu.make_async_copy(level_hbm, level, load_sem.at[4]),
        pltpu.make_async_copy(g_hbm, gate, load_sem.at[5]),
        pltpu.make_async_copy(gain_hbm, gain, load_sem.at[6]),
    ]
    for load in loads:
        load.start()

    barrier = pltpu.get_barrier_semaphore()

    def greet_head(r, _):
        pl.semaphore_signal(
            barrier, inc=1, device_id={"head": lax.rem(me + r, n_head)}, device_id_type=MESH
        )
        return 0

    def greet_seq(r, _):
        pl.semaphore_signal(
            barrier, inc=1, device_id={"seq": lax.rem(seq + r, n_seq)}, device_id_type=MESH
        )
        return 0

    lax.fori_loop(1, n_seq, greet_seq, 0)
    lax.fori_loop(1, n_head, greet_head, 0)

    loads[0].wait()
    lane4 = lax.broadcasted_iota(jnp.int32, (HEADS, CHUNK), 1)
    pieces = []
    for i in range(chunks):
        piece = decay[:, i * CHUNK : (i + 1) * CHUNK]
        for half in range(2):
            begins = doc_ref[seq * (tokens // SPAN) + 2 * i + half] != 0
            drop = jnp.where(begins, RESET, 0.0)
            piece = piece - jnp.where(lane4 == half * SPAN, drop, 0.0)
        pieces.append(piece)
    run = jnp.concatenate(pieces, axis=0)
    lane = lax.broadcasted_iota(jnp.int32, run.shape, 1)
    shift = 1
    while shift < CHUNK:
        run = run + jnp.where(lane >= shift, pltpu.roll(run, shift, 1), 0.0)
        shift *= 2
    total = jnp.broadcast_to(run[:, CHUNK - 1 : CHUNK], run.shape)
    ds[...] = jnp.zeros_like(ds)
    before = jnp.zeros((HEADS, CHUNK), F32)
    after = jnp.zeros((HEADS, CHUNK), F32)
    for i in range(chunks):
        part = slice(i * HEADS, (i + 1) * HEADS)
        ds[i, 0:HEADS, :] = run[part]
        tot[i] = total[part]
        query_w[i] = jnp.exp(before + run[part])
        before = before + total[part]
    for i in reversed(range(chunks)):
        part = slice(i * HEADS, (i + 1) * HEADS)
        key_w[i] = jnp.exp(after + (total[part] - run[part]))
        after = after + total[part]
    own_decay[...] = jnp.zeros_like(own_decay)
    own_decay[0:HEADS, :] = before

    def scaled(i, weights):
        parts = [
            value_t[i, h * DIM : (h + 1) * DIM, :].astype(F32) * weights[h : h + 1, :]
            for h in range(HEADS)
        ]
        return jnp.concatenate(parts, axis=0).astype(BF16)

    def at(i):
        return pl.ds(pl.multiple_of(i * CHUNK, CHUNK), CHUNK)

    loads[2].wait()
    wide[...] = pair[0].reshape(2 * tokens, STATE).astype(F32)
    keys[...] = wide[pl.ds(lax.rem(group, 2), tokens, stride=2), :].astype(BF16)
    loads[1].wait()
    own_state[...] = jnp.zeros_like(own_state)

    def state_step(i, _):
        value_t[i] = raw[at(i), :].T
        own_state[...] += dot(scaled(i, key_w[i]), keys[at(i), :])
        return 0

    lax.fori_loop(0, chunks, state_step, 0)

    pl.semaphore_wait(barrier, n_seq - 1 + n_head - 1)

    swap = pltpu.make_async_remote_copy(
        src_ref=own_state, dst_ref=sib_state, send_sem=swap_sem.at[0], recv_sem=swap_sem.at[1],
        device_id={"seq": 2 * z + 1 - core}, device_id_type=MESH,
    )
    swap.start()

    def decay_copy(other, slot):
        return pltpu.make_async_remote_copy(
            src_ref=own_decay, dst_ref=all_decay.at[slot], send_sem=decay_send.at[other],
            recv_sem=decay_recv.at[slot], device_id={"seq": other}, device_id_type=MESH,
        )

    def send_decay(r, _):
        decay_copy(lax.rem(seq + r, n_seq), seq).start()
        return 0

    lax.fori_loop(1, n_seq, send_decay, 0)
    all_decay[pl.ds(seq, 1)] = own_decay[...][None]

    loads[3].wait()
    wide[...] = pair[1].reshape(2 * tokens, STATE).astype(F32)

    def turn_queries(i, _):
        start = lax.rem(group, 2) + i * (2 * CHUNK)
        query_t[i] = wide[pl.ds(start, CHUNK, stride=2), :].T.astype(BF16)
        return 0

    lax.fori_loop(0, chunks, turn_queries, 0)

    def wait_decay(r, _):
        other = lax.rem(seq + r, n_seq)
        decay_copy(other, other).wait_recv()
        return 0

    lax.fori_loop(1, n_seq, wait_decay, 0)
    swap.wait_recv()

    is_upper = core == 1
    upper_decay = all_decay[2 * z + 1]
    through = jnp.exp(upper_decay)
    mine = pl.ds(pl.multiple_of(core * DIM, DIM), DIM)
    theirs = pl.ds(pl.multiple_of((1 - core) * DIM, DIM), DIM)
    for p in range(PAIRS):
        rows = pl.ds(pl.multiple_of(p * 2 * DIM + core * DIM, DIM), DIM)
        fade = jnp.where(is_upper, through[2 * p + 1 : 2 * p + 2, :], through[2 * p : 2 * p + 1, :])
        here, there = own_state[rows, :], sib_state[rows, :]
        low = jnp.where(is_upper, there, here)
        high = jnp.where(is_upper, here, there)
        chip_state[p] = (low * fade + high).astype(BF16)

    def chip_copy(p, other, slot):
        return pltpu.make_async_remote_copy(
            src_ref=chip_state.at[p], dst_ref=chip_states.at[p, slot],
            send_sem=chip_send.at[p, other], recv_sem=chip_recv.at[p, slot],
            device_id={"seq": 2 * other + core}, device_id_type=MESH,
        )

    for p in range(PAIRS):

        def send_chip(r, _):
            chip_copy(p, lax.rem(z + r, n_z), z).start()
            return 0

        lax.fori_loop(1, n_z, send_chip, 0)

    gap = jnp.zeros((8, CHUNK), F32)
    for j in reversed(range(n_z)):
        coef[j] = jnp.where(j < z, jnp.exp(gap), 0.0)
        gap = gap + jnp.where(j < z, all_decay[2 * j] + all_decay[2 * j + 1], 0.0)
    for p in range(PAIRS):
        rows = slice(p * 2 * DIM, (p + 1) * 2 * DIM)
        levels[p, 0] = jnp.where(is_upper, sib_state[rows, :], 0.0).astype(BF16)

    loads[4].wait()
    loads[5].wait()
    acc[...] = jnp.zeros_like(acc)
    sub_i = lax.broadcasted_iota(jnp.int32, (CHUNK, CHUNK), 0)
    lane_i = lax.broadcasted_iota(jnp.int32, (CHUNK, CHUNK), 1)
    causal = sub_i <= lane_i
    early = sub_i < SPAN
    first_half = lax.broadcasted_iota(jnp.int32, (1, CHUNK), 1) < SPAN
    local_levels = acc.shape[0]

    def near_step(i, _):
        g = gate[at(i), :].astype(F32)
        silu[at(i), :] = g / (1.0 + jnp.exp(-g))
        turned = query_t[i]
        block = keys[at(i), :]
        scores = dot(block, turned)
        run_i = ds[i]
        columns = run_i.T
        weight = jnp.exp(run_i)
        tot_i = tot[i]
        into = dot(
            acc[...].reshape(local_levels * width, STATE).astype(BF16), turned
        ).reshape(local_levels, width, CHUNK)
        for h in range(HEADS):
            rows = slice(h * DIM, (h + 1) * DIM)
            fall = run_i[h : h + 1, :] - jnp.broadcast_to(columns[:, h : h + 1], (CHUNK, CHUNK))
            same = level[0, h : h + 1, at(i)]
            cross = jnp.where(first_half, same, level[1, h : h + 1, at(i)])
            mixed = jnp.exp(jnp.where(causal, fall, -1e30)) * jnp.where(early, cross, same) * scores
            result = dot(value_t[i, rows, :], mixed.astype(BF16))
            for k in range(local_levels):
                on = (lax.shift_right_logical(i, k) & 1).astype(F32)
                factor = level[2 + k, h : h + 1, at(i)] * weight[h : h + 1, :] * on
                result = result + into[k, rows, :] * factor
            near[i, rows, :] = result
        state = dot(scaled(i, jnp.exp(tot_i - run_i[0:HEADS])), block)
        keep = jnp.exp(tot_i)
        for k in range(local_levels):
            low = (1 - (lax.shift_right_logical(i, k) & 1)).astype(F32)
            held = (lax.rem(i, 2 ** (k + 1)) != 0).astype(F32)
            for h in range(HEADS):
                rows = slice(h * DIM, (h + 1) * DIM)
                acc[k, rows, :] = acc[k, rows, :] * (keep[h : h + 1, :] * held) + state[rows, :] * low
        return 0

    lax.fori_loop(0, chunks, near_step, 0)

    def row_copy(p, target, source):
        return pltpu.make_async_remote_copy(
            src_ref=outgoing.at[p, pl.ds(pl.multiple_of(target * rows_out, rows_out), rows_out), :],
            dst_ref=arrived.at[:, pl.ds(pl.multiple_of(source * width + p * CHUNK, CHUNK), CHUNK)],
            send_sem=rows_send.at[p, target], recv_sem=rows_recv.at[p, source],
            device_id={"head": target}, device_id_type=MESH,
        )

    wide_chunk = 2 * CHUNK
    per_chunk = wide_chunk // rows_out
    own_chunk = me // per_chunk
    base = level.shape[0] - far_levels
    shares = []
    beyond = jnp.where(is_upper, jnp.exp(all_decay[2 * z])[0:HEADS], 1.0)

    for p in range(PAIRS):
        def wait_chip(r, _):
            other = lax.rem(z + r, n_z)
            chip_copy(p, other, other).wait_recv()
            return 0

        lax.fori_loop(1, n_z, wait_chip, 0)
        for k in range(far_levels - 1):
            first = (lax.shift_right_logical(z, k) ^ 1) * 2**k
            sums = jnp.zeros((DIM, STATE), F32)
            for n in range(2**k):
                row = coef[first + n]
                fade = jnp.where(is_upper, row[2 * p + 1 : 2 * p + 2, :], row[2 * p : 2 * p + 1, :])
                sums = sums + chip_states[p, first + n].astype(F32) * fade
            own_levels[p, k] = sums.astype(BF16)
        share = pltpu.make_async_remote_copy(
            src_ref=own_levels.at[p], dst_ref=sib_levels.at[p], send_sem=swap_sem.at[2 + 2 * p],
            recv_sem=swap_sem.at[3 + 2 * p], device_id={"seq": 2 * z + 1 - core},
            device_id_type=MESH,
        )
        share.start()
        shares.append(share)
        for k in range(far_levels - 1):
            levels[p, 1 + k, mine, :] = own_levels[p, k]
        share.wait_recv()
        for k in range(far_levels - 1):
            levels[p, 1 + k, theirs, :] = sib_levels[p, k]

        def far_step(r, _):
            i = lax.rem(own_chunk + r, chunks // 2)
            tokens_i = pl.ds(pl.multiple_of(i * wide_chunk, wide_chunk), wide_chunk)
            queries = jnp.concatenate([query_t[2 * i], query_t[2 * i + 1]], axis=1)
            into = dot(
                levels[p].reshape(far_levels * 2 * DIM, STATE), queries
            ).reshape(far_levels, 2 * DIM, wide_chunk)
            weights = [query_w[2 * i], query_w[2 * i + 1]]
            weight = jnp.concatenate(weights, axis=1)
            further = jnp.concatenate([w * beyond for w in weights], axis=1)
            columns = []
            for j in range(2):
                h = 2 * p + j
                rows = slice(h * DIM, (h + 1) * DIM)
                result = jnp.concatenate([near[2 * i, rows, :], near[2 * i + 1, rows, :]], axis=1)
                for k in range(far_levels):
                    from_start = weight if k == 0 else further
                    factor = level[base + k, h : h + 1, tokens_i] * from_start[h : h + 1, :]
                    result = result + into[k, j * DIM : (j + 1) * DIM, :] * factor
                columns.append(result)
            mixed = jnp.concatenate(columns, axis=0).T
            gates = silu[tokens_i, p * CHUNK : (p + 1) * CHUNK]
            outgoing[p, tokens_i, :] = (mixed * gates).astype(BF16)

            def send_rows(k, _):
                target = i * per_chunk + lax.rem(me + k, per_chunk)

                @pl.when(target != me)
                def _():
                    row_copy(p, target, me).start()

                return 0

            lax.fori_loop(0, per_chunk, send_rows, 0)
            return 0

        lax.fori_loop(0, chunks // 2, far_step, 0)
        arrived[:, pl.ds(pl.multiple_of(me * width + p * CHUNK, CHUNK), CHUNK)] = outgoing[
            p, pl.ds(pl.multiple_of(me * rows_out, rows_out), rows_out), :
        ]

    loads[6].wait()
    group_width = PER_GROUP * DIM
    per_group = group_width // width
    groups = n_head // per_group

    def norm_step(r, _):
        g = lax.rem(me // per_group - r + groups, groups)
        for k in range(per_group):
            source = g * per_group + k

            @pl.when(source != me)
            def _():
                for p in range(PAIRS):
                    row_copy(p, source, source).wait_recv()

        x = arrived[:, pl.ds(pl.multiple_of(g * group_width, group_width), group_width)].astype(F32)
        inverse = lax.rsqrt(jnp.sum(x * x, axis=1, keepdims=True) * (1.0 / group_width) + 1e-05)
        for k in range(group_width // CHUNK):
            y = x[:, k * CHUNK : (k + 1) * CHUNK] * inverse * gain[pl.ds(g * (group_width // CHUNK) + k, 1), :]
            out_ref[:, pl.ds(pl.multiple_of(g * group_width + k * CHUNK, CHUNK), CHUNK)] = y.astype(BF16)
        return 0

    lax.fori_loop(0, groups, norm_step, 0)

    def drain_rows(r, _):
        for p in range(PAIRS):
            row_copy(p, lax.rem(me + r, n_head), me).wait_send()
        return 0

    lax.fori_loop(1, n_head, drain_rows, 0)

    def drain_decay(r, _):
        decay_copy(lax.rem(seq + r, n_seq), seq).wait_send()
        return 0

    lax.fori_loop(1, n_seq, drain_decay, 0)

    def drain_chip(r, _):
        for p in range(PAIRS):
            chip_copy(p, lax.rem(z + r, n_z), z).wait_send()
        return 0

    lax.fori_loop(1, n_z, drain_chip, 0)
    swap.wait_send()
    for share in shares:
        share.wait_send()


def solution(mesh):
    n_seq, n_head = mesh.shape["seq"], mesh.shape["head"]
    n_z = n_seq // 2

    def body(values, gate_z, b_keys, c_queries, log_decay, level_weight, doc_start, norm_gain):
        tokens, width = values.shape
        chunks = tokens // CHUNK
        n_levels = level_weight.shape[2]
        far_levels = n_z.bit_length()
        local_levels = chunks.bit_length() - 1
        groups = b_keys.shape[1]
        any_space = pl.BlockSpec(memory_space=pl.ANY)
        rows = tokens // n_head
        dma = pltpu.SemaphoreType.DMA

        def run(*args):
            return kernel(n_seq, n_head, *args)

        return pl.pallas_call(
            run,
            out_shape=jax.ShapeDtypeStruct((rows, n_head * width), BF16),
            in_specs=[any_space] * 7 + [pl.BlockSpec(memory_space=pltpu.SMEM)],
            out_specs=pl.BlockSpec(memory_space=pltpu.VMEM),
            scratch_shapes=[
                pltpu.VMEM((2, tokens, 2, STATE), BF16),
                pltpu.VMEM((2 * tokens, STATE), F32),
                pltpu.VMEM((tokens, STATE), BF16),
                pltpu.VMEM((chunks, STATE, CHUNK), BF16),
                pltpu.VMEM((tokens, width), BF16),
                pltpu.VMEM((chunks, width, CHUNK), BF16),
                pltpu.VMEM((tokens, width), BF16),
                pltpu.VMEM((tokens, width), F32),
                pltpu.VMEM((HEADS, tokens), F32),
                pltpu.VMEM((n_levels, HEADS, tokens), F32),
                pltpu.VMEM((n_head * width // CHUNK, CHUNK), F32),
                pltpu.VMEM((chunks, 8, CHUNK), F32),
                pltpu.VMEM((chunks, HEADS, CHUNK), F32),
                pltpu.VMEM((chunks, HEADS, CHUNK), F32),
                pltpu.VMEM((chunks, HEADS, CHUNK), F32),
                pltpu.VMEM((chunks, width, CHUNK), F32),
                pltpu.VMEM((local_levels, width, STATE), F32),
                pltpu.VMEM((width, STATE), F32),
                pltpu.VMEM((width, STATE), F32),
                pltpu.VMEM((8, CHUNK), F32),
                pltpu.VMEM((n_seq, 8, CHUNK), F32),
                pltpu.VMEM((PAIRS, DIM, STATE), BF16),
                pltpu.VMEM((PAIRS, n_z, DIM, STATE), BF16),
                pltpu.VMEM((n_z, 8, CHUNK), F32),
                pltpu.VMEM((PAIRS, far_levels - 1, DIM, STATE), BF16),
                pltpu.VMEM((PAIRS, far_levels - 1, DIM, STATE), BF16),
                pltpu.VMEM((PAIRS, far_levels, 2 * DIM, STATE), BF16),
                pltpu.VMEM((PAIRS, tokens, CHUNK), BF16),
                pltpu.VMEM((rows, n_head * width), BF16),
                dma((7,)),
                dma((2 + 2 * PAIRS,)),
                dma((n_seq,)),
                dma((n_seq,)),
                dma((PAIRS, n_z)),
                dma((PAIRS, n_z)),
                dma((PAIRS, n_head)),
                dma((PAIRS, n_head)),
            ],
            compiler_params=pltpu.CompilerParams(collective_id=0, has_side_effects=True),
        )(
            b_keys.reshape(tokens, groups // 2, 2, STATE),
            c_queries.reshape(tokens, groups // 2, 2, STATE),
            values,
            gate_z,
            log_decay.T,
            level_weight.transpose(2, 1, 0),
            norm_gain.reshape(n_head * width // CHUNK, CHUNK),
            doc_start,
        )

    in_specs = (
        P("seq", "head"),
        P("seq", "head"),
        P("seq", None, None),
        P("seq", None, None),
        P("seq", "head"),
        P("seq", "head", None),
        P(),
        P(),
    )
    out_specs = P(("seq", "head"), None)
    return jax.shard_map(body, mesh=mesh, in_specs=in_specs, out_specs=out_specs, check_vma=False)
```

```python
import jax
import jax.numpy as jnp
from jax import lax
from jax.experimental import pallas as pl
from jax.experimental.pallas import tpu as pltpu
from jax.sharding import PartitionSpec as P

MESH = pl.DeviceIdType.MESH
F32 = jnp.float32
BF16 = jnp.bfloat16
CHUNK = 128
SPAN = 64
HEADS = 4
DIM = 64
STATE = 128
PER_GROUP = 16
PAIRS = HEADS // 2
RESET = 128.0


def dot(a, b):
    return jnp.dot(a, b, preferred_element_type=F32)


def kernel(
    n_seq, n_head, b_hbm, c_hbm, v_hbm, g_hbm, decay_hbm, level_hbm, gain_hbm, doc_ref, out_ref,
    pair, wide, keys, query_t, raw, value_t, gate, silu, decay, level, gain,
    ds, tot, key_w, query_w, near, acc, own_state, sib_state, own_decay, all_decay,
    chip_state, chip_states, coef, own_levels, sib_levels, levels, outgoing, arrived,
    load_sem, swap_sem, decay_send, decay_recv, chip_send, chip_recv, rows_send, rows_recv,
):
    me = lax.axis_index("head")
    seq = lax.axis_index("seq")
    z, core = seq // 2, lax.rem(seq, 2)
    n_z = n_seq // 2
    far_levels = n_z.bit_length()
    group = me * HEADS // PER_GROUP
    tokens = v_hbm.shape[0]
    chunks = tokens // CHUNK
    width = HEADS * DIM
    rows_out = tokens // n_head

    loads = [
        pltpu.make_async_copy(decay_hbm, decay, load_sem.at[0]),
        pltpu.make_async_copy(v_hbm, raw, load_sem.at[1]),
        pltpu.make_async_copy(b_hbm.at[:, group // 2], pair.at[0], load_sem.at[2]),
        pltpu.make_async_copy(c_hbm.at[:, group // 2], pair.at[1], load_sem.at[3]),
        pltpu.make_async_copy(level_hbm, level, load_sem.at[4]),
        pltpu.make_async_copy(g_hbm, gate, load_sem.at[5]),
        pltpu.make_async_copy(gain_hbm, gain, load_sem.at[6]),
    ]
    for load in loads:
        load.start()

    barrier = pltpu.get_barrier_semaphore()

    def greet_head(r, _):
        pl.semaphore_signal(
            barrier, inc=1, device_id={"head": lax.rem(me + r, n_head)}, device_id_type=MESH
        )
        return 0

    def greet_seq(r, _):
        pl.semaphore_signal(
            barrier, inc=1, device_id={"seq": lax.rem(seq + r, n_seq)}, device_id_type=MESH
        )
        return 0

    lax.fori_loop(1, n_seq, greet_seq, 0)
    lax.fori_loop(1, n_head, greet_head, 0)

    loads[0].wait()
    lane4 = lax.broadcasted_iota(jnp.int32, (HEADS, CHUNK), 1)
    pieces = []
    for i in range(chunks):
        piece = decay[:, i * CHUNK : (i + 1) * CHUNK]
        for half in range(2):
            begins = doc_ref[seq * (tokens // SPAN) + 2 * i + half] != 0
            drop = jnp.where(begins, RESET, 0.0)
            piece = piece - jnp.where(lane4 == half * SPAN, drop, 0.0)
        pieces.append(piece)
    run = jnp.concatenate(pieces, axis=0)
    lane = lax.broadcasted_iota(jnp.int32, run.shape, 1)
    shift = 1
    while shift < CHUNK:
        run = run + jnp.where(lane >= shift, pltpu.roll(run, shift, 1), 0.0)
        shift *= 2
    total = jnp.broadcast_to(run[:, CHUNK - 1 : CHUNK], run.shape)
    ds[...] = jnp.zeros_like(ds)
    before = jnp.zeros((HEADS, CHUNK), F32)
    after = jnp.zeros((HEADS, CHUNK), F32)
    for i in range(chunks):
        part = slice(i * HEADS, (i + 1) * HEADS)
        ds[i, 0:HEADS, :] = run[part]
        tot[i] = total[part]
        query_w[i] = jnp.exp(before + run[part])
        before = before + total[part]
    for i in reversed(range(chunks)):
        part = slice(i * HEADS, (i + 1) * HEADS)
        key_w[i] = jnp.exp(after + (total[part] - run[part]))
        after = after + total[part]
    own_decay[...] = jnp.zeros_like(own_decay)
    own_decay[0:HEADS, :] = before

    def scaled(i, weights):
        parts = [
            value_t[i, h * DIM : (h + 1) * DIM, :].astype(F32) * weights[h : h + 1, :]
            for h in range(HEADS)
        ]
        return jnp.concatenate(parts, axis=0).astype(BF16)

    def at(i):
        return pl.ds(pl.multiple_of(i * CHUNK, CHUNK), CHUNK)

    loads[2].wait()
    wide[...] = pair[0].reshape(2 * tokens, STATE).astype(F32)
    keys[...] = wide[pl.ds(lax.rem(group, 2), tokens, stride=2), :].astype(BF16)
    loads[1].wait()
    own_state[...] = jnp.zeros_like(own_state)

    def state_step(i, _):
        value_t[i] = raw[at(i), :].T
        own_state[...] += dot(scaled(i, key_w[i]), keys[at(i), :])
        return 0

    lax.fori_loop(0, chunks, state_step, 0)

    pl.semaphore_wait(barrier, n_seq - 1 + n_head - 1)

    swap = pltpu.make_async_remote_copy(
        src_ref=own_state, dst_ref=sib_state, send_sem=swap_sem.at[0], recv_sem=swap_sem.at[1],
        device_id={"seq": 2 * z + 1 - core}, device_id_type=MESH,
    )
    swap.start()

    def decay_copy(other, slot):
        return pltpu.make_async_remote_copy(
            src_ref=own_decay, dst_ref=all_decay.at[slot], send_sem=decay_send.at[other],
            recv_sem=decay_recv.at[slot], device_id={"seq": other}, device_id_type=MESH,
        )

    def send_decay(r, _):
        decay_copy(lax.rem(seq + r, n_seq), seq).start()
        return 0

    lax.fori_loop(1, n_seq, send_decay, 0)
    all_decay[pl.ds(seq, 1)] = own_decay[...][None]

    loads[3].wait()
    wide[...] = pair[1].reshape(2 * tokens, STATE).astype(F32)

    def turn_queries(i, _):
        start = lax.rem(group, 2) + i * (2 * CHUNK)
        query_t[i] = wide[pl.ds(start, CHUNK, stride=2), :].T.astype(BF16)
        return 0

    lax.fori_loop(0, chunks, turn_queries, 0)

    sibling = 2 * z + 1 - core
    decay_copy(sibling, sibling).wait_recv()
    swap.wait_recv()

    is_upper = core == 1
    upper_decay = all_decay[2 * z + 1]
    through = jnp.exp(upper_decay)
    mine = pl.ds(pl.multiple_of(core * DIM, DIM), DIM)
    theirs = pl.ds(pl.multiple_of((1 - core) * DIM, DIM), DIM)
    for p in range(PAIRS):
        rows = pl.ds(pl.multiple_of(p * 2 * DIM + core * DIM, DIM), DIM)
        fade = jnp.where(is_upper, through[2 * p + 1 : 2 * p + 2, :], through[2 * p : 2 * p + 1, :])
        here, there = own_state[rows, :], sib_state[rows, :]
        low = jnp.where(is_upper, there, here)
        high = jnp.where(is_upper, here, there)
        chip_state[p] = (low * fade + high).astype(BF16)

    def chip_copy(p, other, slot):
        return pltpu.make_async_remote_copy(
            src_ref=chip_state.at[p], dst_ref=chip_states.at[p, slot],
            send_sem=chip_send.at[p, other], recv_sem=chip_recv.at[p, slot],
            device_id={"seq": 2 * other + core}, device_id_type=MESH,
        )

    def send_chips(p):
        def send_chip(r, _):
            chip_copy(p, lax.rem(z + r, n_z), z).start()
            return 0

        lax.fori_loop(1, n_z, send_chip, 0)

    send_chips(0)
    for p in range(PAIRS):
        rows = slice(p * 2 * DIM, (p + 1) * 2 * DIM)
        levels[p, 0] = jnp.where(is_upper, sib_state[rows, :], 0.0).astype(BF16)

    loads[4].wait()
    loads[5].wait()
    acc[...] = jnp.zeros_like(acc)
    sub_i = lax.broadcasted_iota(jnp.int32, (CHUNK, CHUNK), 0)
    lane_i = lax.broadcasted_iota(jnp.int32, (CHUNK, CHUNK), 1)
    causal = sub_i <= lane_i
    early = sub_i < SPAN
    first_half = lax.broadcasted_iota(jnp.int32, (1, CHUNK), 1) < SPAN
    local_levels = acc.shape[0]

    def near_step(i, _):
        g = gate[at(i), :].astype(F32)
        silu[at(i), :] = g / (1.0 + jnp.exp(-g))
        turned = query_t[i]
        block = keys[at(i), :]
        scores = dot(block, turned)
        run_i = ds[i]
        columns = run_i.T
        weight = jnp.exp(run_i)
        tot_i = tot[i]
        into = dot(
            acc[...].reshape(local_levels * width, STATE).astype(BF16), turned
        ).reshape(local_levels, width, CHUNK)
        for h in range(HEADS):
            rows = slice(h * DIM, (h + 1) * DIM)
            fall = run_i[h : h + 1, :] - jnp.broadcast_to(columns[:, h : h + 1], (CHUNK, CHUNK))
            same = level[0, h : h + 1, at(i)]
            cross = jnp.where(first_half, same, level[1, h : h + 1, at(i)])
            mixed = jnp.exp(jnp.where(causal, fall, -1e30)) * jnp.where(early, cross, same) * scores
            result = dot(value_t[i, rows, :], mixed.astype(BF16))
            for k in range(local_levels):
                on = (lax.shift_right_logical(i, k) & 1).astype(F32)
                factor = level[2 + k, h : h + 1, at(i)] * weight[h : h + 1, :] * on
                result = result + into[k, rows, :] * factor
            near[i, rows, :] = result
        state = dot(scaled(i, jnp.exp(tot_i - run_i[0:HEADS])), block)
        keep = jnp.exp(tot_i)
        for k in range(local_levels):
            low = (1 - (lax.shift_right_logical(i, k) & 1)).astype(F32)
            held = (lax.rem(i, 2 ** (k + 1)) != 0).astype(F32)
            for h in range(HEADS):
                rows = slice(h * DIM, (h + 1) * DIM)
                acc[k, rows, :] = acc[k, rows, :] * (keep[h : h + 1, :] * held) + state[rows, :] * low
        return 0

    lax.fori_loop(0, chunks, near_step, 0)
    for p in range(1, PAIRS):
        send_chips(p)

    def wait_decay(r, _):
        other = lax.rem(seq + r, n_seq)

        @pl.when(other != sibling)
        def _():
            decay_copy(other, other).wait_recv()

        return 0

    lax.fori_loop(1, n_seq, wait_decay, 0)
    gap = jnp.zeros((8, CHUNK), F32)
    for j in reversed(range(n_z)):
        coef[j] = jnp.where(j < z, jnp.exp(gap), 0.0)
        gap = gap + jnp.where(j < z, all_decay[2 * j] + all_decay[2 * j + 1], 0.0)

    def row_copy(p, target, source):
        return pltpu.make_async_remote_copy(
            src_ref=outgoing.at[p, pl.ds(pl.multiple_of(target * rows_out, rows_out), rows_out), :],
            dst_ref=arrived.at[:, pl.ds(pl.multiple_of(source * width + p * CHUNK, CHUNK), CHUNK)],
            send_sem=rows_send.at[p, target], recv_sem=rows_recv.at[p, source],
            device_id={"head": target}, device_id_type=MESH,
        )

    wide_chunk = 2 * CHUNK
    per_chunk = wide_chunk // rows_out
    own_chunk = me // per_chunk
    base = level.shape[0] - far_levels
    shares = []
    beyond = jnp.where(is_upper, jnp.exp(all_decay[2 * z])[0:HEADS], 1.0)

    for p in range(PAIRS):
        def wait_chip(r, _):
            other = lax.rem(z + r, n_z)
            chip_copy(p, other, other).wait_recv()
            return 0

        lax.fori_loop(1, n_z, wait_chip, 0)
        for k in range(far_levels - 1):
            first = (lax.shift_right_logical(z, k) ^ 1) * 2**k
            sums = jnp.zeros((DIM, STATE), F32)
            for n in range(2**k):
                row = coef[first + n]
                fade = jnp.where(is_upper, row[2 * p + 1 : 2 * p + 2, :], row[2 * p : 2 * p + 1, :])
                sums = sums + chip_states[p, first + n].astype(F32) * fade
            own_levels[p, k] = sums.astype(BF16)
        share = pltpu.make_async_remote_copy(
            src_ref=own_levels.at[p], dst_ref=sib_levels.at[p], send_sem=swap_sem.at[2 + 2 * p],
            recv_sem=swap_sem.at[3 + 2 * p], device_id={"seq": 2 * z + 1 - core},
            device_id_type=MESH,
        )
        share.start()
        shares.append(share)
        for k in range(far_levels - 1):
            levels[p, 1 + k, mine, :] = own_levels[p, k]
        share.wait_recv()
        for k in range(far_levels - 1):
            levels[p, 1 + k, theirs, :] = sib_levels[p, k]

        def far_step(r, _):
            i = lax.rem(own_chunk + r, chunks // 2)
            tokens_i = pl.ds(pl.multiple_of(i * wide_chunk, wide_chunk), wide_chunk)
            queries = jnp.concatenate([query_t[2 * i], query_t[2 * i + 1]], axis=1)
            into = dot(
                levels[p].reshape(far_levels * 2 * DIM, STATE), queries
            ).reshape(far_levels, 2 * DIM, wide_chunk)
            weights = [query_w[2 * i], query_w[2 * i + 1]]
            weight = jnp.concatenate(weights, axis=1)
            further = jnp.concatenate([w * beyond for w in weights], axis=1)
            columns = []
            for j in range(2):
                h = 2 * p + j
                rows = slice(h * DIM, (h + 1) * DIM)
                result = jnp.concatenate([near[2 * i, rows, :], near[2 * i + 1, rows, :]], axis=1)
                for k in range(far_levels):
                    from_start = weight if k == 0 else further
                    factor = level[base + k, h : h + 1, tokens_i] * from_start[h : h + 1, :]
                    result = result + into[k, j * DIM : (j + 1) * DIM, :] * factor
                columns.append(result)
            mixed = jnp.concatenate(columns, axis=0).T
            gates = silu[tokens_i, p * CHUNK : (p + 1) * CHUNK]
            outgoing[p, tokens_i, :] = (mixed * gates).astype(BF16)

            def send_rows(k, _):
                target = i * per_chunk + lax.rem(me + k, per_chunk)

                @pl.when(target != me)
                def _():
                    row_copy(p, target, me).start()

                return 0

            lax.fori_loop(0, per_chunk, send_rows, 0)
            return 0

        lax.fori_loop(0, chunks // 2, far_step, 0)
        arrived[:, pl.ds(pl.multiple_of(me * width + p * CHUNK, CHUNK), CHUNK)] = outgoing[
            p, pl.ds(pl.multiple_of(me * rows_out, rows_out), rows_out), :
        ]

    loads[6].wait()
    group_width = PER_GROUP * DIM
    per_group = group_width // width
    groups = n_head // per_group

    def norm_step(r, _):
        g = lax.rem(me // per_group - r + groups, groups)
        for k in range(per_group):
            source = g * per_group + k

            @pl.when(source != me)
            def _():
                for p in range(PAIRS):
                    row_copy(p, source, source).wait_recv()

        x = arrived[:, pl.ds(pl.multiple_of(g * group_width, group_width), group_width)].astype(F32)
        inverse = lax.rsqrt(jnp.sum(x * x, axis=1, keepdims=True) * (1.0 / group_width) + 1e-05)
        for k in range(group_width // CHUNK):
            y = x[:, k * CHUNK : (k + 1) * CHUNK] * inverse * gain[pl.ds(g * (group_width // CHUNK) + k, 1), :]
            out_ref[:, pl.ds(pl.multiple_of(g * group_width + k * CHUNK, CHUNK), CHUNK)] = y.astype(BF16)
        return 0

    lax.fori_loop(0, groups, norm_step, 0)

    def drain_rows(r, _):
        for p in range(PAIRS):
            row_copy(p, lax.rem(me + r, n_head), me).wait_send()
        return 0

    lax.fori_loop(1, n_head, drain_rows, 0)

    def drain_decay(r, _):
        decay_copy(lax.rem(seq + r, n_seq), seq).wait_send()
        return 0

    lax.fori_loop(1, n_seq, drain_decay, 0)

    def drain_chip(r, _):
        for p in range(PAIRS):
            chip_copy(p, lax.rem(z + r, n_z), z).wait_send()
        return 0

    lax.fori_loop(1, n_z, drain_chip, 0)
    swap.wait_send()
    for share in shares:
        share.wait_send()


def solution(mesh):
    n_seq, n_head = mesh.shape["seq"], mesh.shape["head"]
    n_z = n_seq // 2

    def body(values, gate_z, b_keys, c_queries, log_decay, level_weight, doc_start, norm_gain):
        tokens, width = values.shape
        chunks = tokens // CHUNK
        n_levels = level_weight.shape[2]
        far_levels = n_z.bit_length()
        local_levels = chunks.bit_length() - 1
        groups = b_keys.shape[1]
        any_space = pl.BlockSpec(memory_space=pl.ANY)
        rows = tokens // n_head
        dma = pltpu.SemaphoreType.DMA

        def run(*args):
            return kernel(n_seq, n_head, *args)

        return pl.pallas_call(
            run,
            out_shape=jax.ShapeDtypeStruct((rows, n_head * width), BF16),
            in_specs=[any_space] * 7 + [pl.BlockSpec(memory_space=pltpu.SMEM)],
            out_specs=pl.BlockSpec(memory_space=pltpu.VMEM),
            scratch_shapes=[
                pltpu.VMEM((2, tokens, 2, STATE), BF16),
                pltpu.VMEM((2 * tokens, STATE), F32),
                pltpu.VMEM((tokens, STATE), BF16),
                pltpu.VMEM((chunks, STATE, CHUNK), BF16),
                pltpu.VMEM((tokens, width), BF16),
                pltpu.VMEM((chunks, width, CHUNK), BF16),
                pltpu.VMEM((tokens, width), BF16),
                pltpu.VMEM((tokens, width), F32),
                pltpu.VMEM((HEADS, tokens), F32),
                pltpu.VMEM((n_levels, HEADS, tokens), F32),
                pltpu.VMEM((n_head * width // CHUNK, CHUNK), F32),
                pltpu.VMEM((chunks, 8, CHUNK), F32),
                pltpu.VMEM((chunks, HEADS, CHUNK), F32),
                pltpu.VMEM((chunks, HEADS, CHUNK), F32),
                pltpu.VMEM((chunks, HEADS, CHUNK), F32),
                pltpu.VMEM((chunks, width, CHUNK), F32),
                pltpu.VMEM((local_levels, width, STATE), F32),
                pltpu.VMEM((width, STATE), F32),
                pltpu.VMEM((width, STATE), F32),
                pltpu.VMEM((8, CHUNK), F32),
                pltpu.VMEM((n_seq, 8, CHUNK), F32),
                pltpu.VMEM((PAIRS, DIM, STATE), BF16),
                pltpu.VMEM((PAIRS, n_z, DIM, STATE), BF16),
                pltpu.VMEM((n_z, 8, CHUNK), F32),
                pltpu.VMEM((PAIRS, far_levels - 1, DIM, STATE), BF16),
                pltpu.VMEM((PAIRS, far_levels - 1, DIM, STATE), BF16),
                pltpu.VMEM((PAIRS, far_levels, 2 * DIM, STATE), BF16),
                pltpu.VMEM((PAIRS, tokens, CHUNK), BF16),
                pltpu.VMEM((rows, n_head * width), BF16),
                dma((7,)),
                dma((2 + 2 * PAIRS,)),
                dma((n_seq,)),
                dma((n_seq,)),
                dma((PAIRS, n_z)),
                dma((PAIRS, n_z)),
                dma((PAIRS, n_head)),
                dma((PAIRS, n_head)),
            ],
            compiler_params=pltpu.CompilerParams(collective_id=0, has_side_effects=True),
        )(
            b_keys.reshape(tokens, groups // 2, 2, STATE),
            c_queries.reshape(tokens, groups // 2, 2, STATE),
            values,
            gate_z,
            log_decay.T,
            level_weight.transpose(2, 1, 0),
            norm_gain.reshape(n_head * width // CHUNK, CHUNK),
            doc_start,
        )

    in_specs = (
        P("seq", "head"),
        P("seq", "head"),
        P("seq", None, None),
        P("seq", None, None),
        P("seq", "head"),
        P("seq", "head", None),
        P(),
        P(),
    )
    out_specs = P(("seq", "head"), None)
    return jax.shard_map(body, mesh=mesh, in_specs=in_specs, out_specs=out_specs, check_vma=False)
```

```python
import jax
import jax.numpy as jnp
from jax import lax
from jax.experimental import pallas as pl
from jax.experimental.pallas import tpu as pltpu
from jax.sharding import PartitionSpec as P

MESH = pl.DeviceIdType.MESH
F32 = jnp.float32
BF16 = jnp.bfloat16
CHUNK = 128
SPAN = 64
HEADS = 4
DIM = 64
STATE = 128
PER_GROUP = 16
PAIRS = HEADS // 2
SECTIONS = 4
RESET = 128.0


def dot(a, b):
    return jnp.dot(a, b, preferred_element_type=F32)


def kernel(
    n_seq, n_head, b_hbm, c_hbm, v_hbm, g_hbm, decay_hbm, level_hbm, doc_ref, out_ref,
    pair, wide, keys, query_t, raw, value_t, gate, silu, decay, level,
    ds, tot, key_w, query_w, near, acc, own_state, sib_state, own_decay, all_decay,
    chip_state, chip_states, coef, own_levels, sib_levels, levels, outgoing, arrived,
    load_sem, swap_sem, decay_send, decay_recv, chip_send, chip_recv, rows_send, rows_recv,
):
    me = lax.axis_index("head")
    seq = lax.axis_index("seq")
    z, core = seq // 2, lax.rem(seq, 2)
    n_z = n_seq // 2
    far_levels = n_z.bit_length()
    group = me * HEADS // PER_GROUP
    tokens = v_hbm.shape[0]
    chunks = tokens // CHUNK
    width = HEADS * DIM
    rows_out = tokens // n_head

    loads = [
        pltpu.make_async_copy(decay_hbm, decay, load_sem.at[0]),
        pltpu.make_async_copy(v_hbm, raw, load_sem.at[1]),
        pltpu.make_async_copy(c_hbm.at[:, group // 2], pair.at[1], load_sem.at[2]),
        pltpu.make_async_copy(level_hbm, level, load_sem.at[3]),
        pltpu.make_async_copy(g_hbm, gate, load_sem.at[4]),
    ]
    section = tokens // SECTIONS
    key_loads = [
        pltpu.make_async_copy(
            b_hbm.at[pl.ds(j * section, section), group // 2],
            pair.at[0, pl.ds(j * section, section)], load_sem.at[5 + j],
        )
        for j in range(SECTIONS)
    ]
    for load in loads[:2] + key_loads + loads[2:]:
        load.start()

    barrier = pltpu.get_barrier_semaphore()

    def greet_head(r, _):
        pl.semaphore_signal(
            barrier, inc=1, device_id={"head": lax.rem(me + r, n_head)}, device_id_type=MESH
        )
        return 0

    def greet_seq(r, _):
        pl.semaphore_signal(
            barrier, inc=1, device_id={"seq": lax.rem(seq + r, n_seq)}, device_id_type=MESH
        )
        return 0

    lax.fori_loop(1, n_seq, greet_seq, 0)
    lax.fori_loop(1, n_head, greet_head, 0)

    loads[0].wait()
    lane4 = lax.broadcasted_iota(jnp.int32, (HEADS, CHUNK), 1)
    pieces = []
    for i in range(chunks):
        piece = decay[:, i * CHUNK : (i + 1) * CHUNK]
        for half in range(2):
            begins = doc_ref[seq * (tokens // SPAN) + 2 * i + half] != 0
            drop = jnp.where(begins, RESET, 0.0)
            piece = piece - jnp.where(lane4 == half * SPAN, drop, 0.0)
        pieces.append(piece)
    run = jnp.concatenate(pieces, axis=0)
    lane = lax.broadcasted_iota(jnp.int32, run.shape, 1)
    shift = 1
    while shift < CHUNK:
        run = run + jnp.where(lane >= shift, pltpu.roll(run, shift, 1), 0.0)
        shift *= 2
    total = jnp.broadcast_to(run[:, CHUNK - 1 : CHUNK], run.shape)
    ds[...] = jnp.zeros_like(ds)
    before = jnp.zeros((HEADS, CHUNK), F32)
    after = jnp.zeros((HEADS, CHUNK), F32)
    for i in range(chunks):
        part = slice(i * HEADS, (i + 1) * HEADS)
        ds[i, 0:HEADS, :] = run[part]
        tot[i] = total[part]
        query_w[i] = jnp.exp(before + run[part])
        before = before + total[part]
    for i in reversed(range(chunks)):
        part = slice(i * HEADS, (i + 1) * HEADS)
        key_w[i] = jnp.exp(after + (total[part] - run[part]))
        after = after + total[part]
    own_decay[...] = jnp.zeros_like(own_decay)
    own_decay[0:HEADS, :] = before

    def scaled(i, weights):
        parts = [
            value_t[i, h * DIM : (h + 1) * DIM, :].astype(F32) * weights[h : h + 1, :]
            for h in range(HEADS)
        ]
        return jnp.concatenate(parts, axis=0).astype(BF16)

    def at(i):
        return pl.ds(pl.multiple_of(i * CHUNK, CHUNK), CHUNK)

    loads[1].wait()
    own_state[...] = jnp.zeros_like(own_state)

    def state_step(i, _):
        value_t[i] = raw[at(i), :].T
        own_state[...] += dot(scaled(i, key_w[i]), keys[at(i), :])
        return 0

    for j in range(SECTIONS):
        rows = slice(j * section, (j + 1) * section)
        key_loads[j].wait()
        both = pair[0, rows].reshape(2 * section, STATE)
        wide[2 * j * section : 2 * (j + 1) * section, :] = both.astype(F32)
        start = lax.rem(group, 2) + 2 * j * section
        keys[rows, :] = wide[pl.ds(start, section, stride=2), :].astype(BF16)
        lax.fori_loop(j * chunks // SECTIONS, (j + 1) * chunks // SECTIONS, state_step, 0)

    pl.semaphore_wait(barrier, n_seq - 1 + n_head - 1)

    swap = pltpu.make_async_remote_copy(
        src_ref=own_state, dst_ref=sib_state, send_sem=swap_sem.at[0], recv_sem=swap_sem.at[1],
        device_id={"seq": 2 * z + 1 - core}, device_id_type=MESH,
    )
    swap.start()

    def decay_copy(other, slot):
        return pltpu.make_async_remote_copy(
            src_ref=own_decay, dst_ref=all_decay.at[slot], send_sem=decay_send.at[other],
            recv_sem=decay_recv.at[slot], device_id={"seq": other}, device_id_type=MESH,
        )

    def send_decay(r, _):
        decay_copy(lax.rem(seq + r, n_seq), seq).start()
        return 0

    lax.fori_loop(1, n_seq, send_decay, 0)
    all_decay[pl.ds(seq, 1)] = own_decay[...][None]

    loads[2].wait()
    wide[...] = pair[1].reshape(2 * tokens, STATE).astype(F32)

    def turn_queries(i, _):
        start = lax.rem(group, 2) + i * (2 * CHUNK)
        query_t[i] = wide[pl.ds(start, CHUNK, stride=2), :].T.astype(BF16)
        return 0

    lax.fori_loop(0, chunks, turn_queries, 0)

    sibling = 2 * z + 1 - core
    decay_copy(sibling, sibling).wait_recv()
    swap.wait_recv()

    is_upper = core == 1
    upper_decay = all_decay[2 * z + 1]
    through = jnp.exp(upper_decay)
    mine = pl.ds(pl.multiple_of(core * DIM, DIM), DIM)
    theirs = pl.ds(pl.multiple_of((1 - core) * DIM, DIM), DIM)
    for p in range(PAIRS):
        rows = pl.ds(pl.multiple_of(p * 2 * DIM + core * DIM, DIM), DIM)
        fade = jnp.where(is_upper, through[2 * p + 1 : 2 * p + 2, :], through[2 * p : 2 * p + 1, :])
        here, there = own_state[rows, :], sib_state[rows, :]
        low = jnp.where(is_upper, there, here)
        high = jnp.where(is_upper, here, there)
        chip_state[p] = (low * fade + high).astype(BF16)

    def chip_copy(p, other, slot):
        return pltpu.make_async_remote_copy(
            src_ref=chip_state.at[p], dst_ref=chip_states.at[p, slot],
            send_sem=chip_send.at[p, other], recv_sem=chip_recv.at[p, slot],
            device_id={"seq": 2 * other + core}, device_id_type=MESH,
        )

    def send_chips(p):
        def send_chip(r, _):
            chip_copy(p, lax.rem(z + r, n_z), z).start()
            return 0

        lax.fori_loop(1, n_z, send_chip, 0)

    send_chips(0)
    for p in range(PAIRS):
        rows = slice(p * 2 * DIM, (p + 1) * 2 * DIM)
        levels[p, 0] = jnp.where(is_upper, sib_state[rows, :], 0.0).astype(BF16)

    loads[3].wait()
    loads[4].wait()
    acc[...] = jnp.zeros_like(acc)
    sub_i = lax.broadcasted_iota(jnp.int32, (CHUNK, CHUNK), 0)
    lane_i = lax.broadcasted_iota(jnp.int32, (CHUNK, CHUNK), 1)
    causal = sub_i <= lane_i
    early = sub_i < SPAN
    first_half = lax.broadcasted_iota(jnp.int32, (1, CHUNK), 1) < SPAN
    local_levels = acc.shape[0]

    def near_step(i, _):
        g = gate[at(i), :].astype(F32)
        silu[at(i), :] = g / (1.0 + jnp.exp(-g))
        turned = query_t[i]
        block = keys[at(i), :]
        scores = dot(block, turned)
        run_i = ds[i]
        columns = run_i.T
        weight = jnp.exp(run_i)
        tot_i = tot[i]
        into = dot(
            acc[...].reshape(local_levels * width, STATE).astype(BF16), turned
        ).reshape(local_levels, width, CHUNK)
        for h in range(HEADS):
            rows = slice(h * DIM, (h + 1) * DIM)
            fall = run_i[h : h + 1, :] - jnp.broadcast_to(columns[:, h : h + 1], (CHUNK, CHUNK))
            same = level[0, h : h + 1, at(i)]
            cross = jnp.where(first_half, same, level[1, h : h + 1, at(i)])
            mixed = jnp.exp(jnp.where(causal, fall, -1e30)) * jnp.where(early, cross, same) * scores
            result = dot(value_t[i, rows, :], mixed.astype(BF16))
            for k in range(local_levels):
                on = (lax.shift_right_logical(i, k) & 1).astype(F32)
                factor = level[2 + k, h : h + 1, at(i)] * weight[h : h + 1, :] * on
                result = result + into[k, rows, :] * factor
            near[i, rows, :] = result
        state = dot(scaled(i, jnp.exp(tot_i - run_i[0:HEADS])), block)
        keep = jnp.exp(tot_i)
        for k in range(local_levels):
            low = (1 - (lax.shift_right_logical(i, k) & 1)).astype(F32)
            held = (lax.rem(i, 2 ** (k + 1)) != 0).astype(F32)
            for h in range(HEADS):
                rows = slice(h * DIM, (h + 1) * DIM)
                acc[k, rows, :] = acc[k, rows, :] * (keep[h : h + 1, :] * held) + state[rows, :] * low
        return 0

    lax.fori_loop(0, chunks, near_step, 0)
    for p in range(1, PAIRS):
        send_chips(p)

    def wait_decay(r, _):
        other = lax.rem(seq + r, n_seq)

        @pl.when(other != sibling)
        def _():
            decay_copy(other, other).wait_recv()

        return 0

    lax.fori_loop(1, n_seq, wait_decay, 0)
    gap = jnp.zeros((8, CHUNK), F32)
    for j in reversed(range(n_z)):
        coef[j] = jnp.where(j < z, jnp.exp(gap), 0.0)
        gap = gap + jnp.where(j < z, all_decay[2 * j] + all_decay[2 * j + 1], 0.0)

    def row_copy(p, target, source):
        return pltpu.make_async_remote_copy(
            src_ref=outgoing.at[p, pl.ds(pl.multiple_of(target * rows_out, rows_out), rows_out), :],
            dst_ref=arrived.at[:, pl.ds(pl.multiple_of(source * width + p * CHUNK, CHUNK), CHUNK)],
            send_sem=rows_send.at[p, target], recv_sem=rows_recv.at[p, source],
            device_id={"head": target}, device_id_type=MESH,
        )

    wide_chunk = 2 * CHUNK
    per_chunk = wide_chunk // rows_out
    own_chunk = me // per_chunk
    base = level.shape[0] - far_levels
    shares = []
    beyond = jnp.where(is_upper, jnp.exp(all_decay[2 * z])[0:HEADS], 1.0)

    for p in range(PAIRS):
        def wait_chip(r, _):
            other = lax.rem(z + r, n_z)
            chip_copy(p, other, other).wait_recv()
            return 0

        lax.fori_loop(1, n_z, wait_chip, 0)
        for k in range(far_levels - 1):
            first = (lax.shift_right_logical(z, k) ^ 1) * 2**k
            sums = jnp.zeros((DIM, STATE), F32)
            for n in range(2**k):
                row = coef[first + n]
                fade = jnp.where(is_upper, row[2 * p + 1 : 2 * p + 2, :], row[2 * p : 2 * p + 1, :])
                sums = sums + chip_states[p, first + n].astype(F32) * fade
            own_levels[p, k] = sums.astype(BF16)
        share = pltpu.make_async_remote_copy(
            src_ref=own_levels.at[p], dst_ref=sib_levels.at[p], send_sem=swap_sem.at[2 + 2 * p],
            recv_sem=swap_sem.at[3 + 2 * p], device_id={"seq": 2 * z + 1 - core},
            device_id_type=MESH,
        )
        share.start()
        shares.append(share)
        for k in range(far_levels - 1):
            levels[p, 1 + k, mine, :] = own_levels[p, k]
        share.wait_recv()
        for k in range(far_levels - 1):
            levels[p, 1 + k, theirs, :] = sib_levels[p, k]

        def far_step(r, _):
            i = lax.rem(own_chunk + r, chunks // 2)
            tokens_i = pl.ds(pl.multiple_of(i * wide_chunk, wide_chunk), wide_chunk)
            queries = jnp.concatenate([query_t[2 * i], query_t[2 * i + 1]], axis=1)
            into = dot(
                levels[p].reshape(far_levels * 2 * DIM, STATE), queries
            ).reshape(far_levels, 2 * DIM, wide_chunk)
            weights = [query_w[2 * i], query_w[2 * i + 1]]
            weight = jnp.concatenate(weights, axis=1)
            further = jnp.concatenate([w * beyond for w in weights], axis=1)
            columns = []
            for j in range(2):
                h = 2 * p + j
                rows = slice(h * DIM, (h + 1) * DIM)
                result = jnp.concatenate([near[2 * i, rows, :], near[2 * i + 1, rows, :]], axis=1)
                for k in range(far_levels):
                    from_start = weight if k == 0 else further
                    factor = level[base + k, h : h + 1, tokens_i] * from_start[h : h + 1, :]
                    result = result + into[k, j * DIM : (j + 1) * DIM, :] * factor
                columns.append(result)
            mixed = jnp.concatenate(columns, axis=0).T
            gates = silu[tokens_i, p * CHUNK : (p + 1) * CHUNK]
            outgoing[p, tokens_i, :] = (mixed * gates).astype(BF16)

            def send_rows(k, _):
                target = i * per_chunk + lax.rem(me + k, per_chunk)

                @pl.when(target != me)
                def _():
                    row_copy(p, target, me).start()

                return 0

            lax.fori_loop(0, per_chunk, send_rows, 0)
            return 0

        lax.fori_loop(0, chunks // 2, far_step, 0)
        arrived[:, pl.ds(pl.multiple_of(me * width + p * CHUNK, CHUNK), CHUNK)] = outgoing[
            p, pl.ds(pl.multiple_of(me * rows_out, rows_out), rows_out), :
        ]

    group_width = PER_GROUP * DIM
    per_group = group_width // width
    groups = n_head // per_group

    def norm_step(r, _):
        g = lax.rem(me // per_group - r + groups, groups)
        for k in range(per_group):
            source = g * per_group + k

            @pl.when(source != me)
            def _():
                for p in range(PAIRS):
                    row_copy(p, source, source).wait_recv()

        x = arrived[:, pl.ds(pl.multiple_of(g * group_width, group_width), group_width)].astype(F32)
        inverse = lax.rsqrt(jnp.sum(x * x, axis=1, keepdims=True) * (1.0 / group_width) + 1e-05)
        for k in range(group_width // CHUNK):
            y = x[:, k * CHUNK : (k + 1) * CHUNK] * inverse
            out_ref[:, pl.ds(pl.multiple_of(g * group_width + k * CHUNK, CHUNK), CHUNK)] = y
        return 0

    lax.fori_loop(0, groups, norm_step, 0)

    def drain_rows(r, _):
        for p in range(PAIRS):
            row_copy(p, lax.rem(me + r, n_head), me).wait_send()
        return 0

    lax.fori_loop(1, n_head, drain_rows, 0)

    def drain_decay(r, _):
        decay_copy(lax.rem(seq + r, n_seq), seq).wait_send()
        return 0

    lax.fori_loop(1, n_seq, drain_decay, 0)

    def drain_chip(r, _):
        for p in range(PAIRS):
            chip_copy(p, lax.rem(z + r, n_z), z).wait_send()
        return 0

    lax.fori_loop(1, n_z, drain_chip, 0)
    swap.wait_send()
    for share in shares:
        share.wait_send()


def solution(mesh):
    n_seq, n_head = mesh.shape["seq"], mesh.shape["head"]
    n_z = n_seq // 2

    def body(values, gate_z, b_keys, c_queries, log_decay, level_weight, doc_start, norm_gain):
        tokens, width = values.shape
        chunks = tokens // CHUNK
        n_levels = level_weight.shape[2]
        far_levels = n_z.bit_length()
        local_levels = chunks.bit_length() - 1
        groups = b_keys.shape[1]
        any_space = pl.BlockSpec(memory_space=pl.ANY)
        rows = tokens // n_head
        dma = pltpu.SemaphoreType.DMA

        def run(*args):
            return kernel(n_seq, n_head, *args)

        whole = pl.pallas_call(
            run,
            out_shape=jax.ShapeDtypeStruct((rows, n_head * width), F32),
            in_specs=[any_space] * 6 + [pl.BlockSpec(memory_space=pltpu.SMEM)],
            out_specs=pl.BlockSpec(memory_space=pltpu.VMEM),
            scratch_shapes=[
                pltpu.VMEM((2, tokens, 2, STATE), BF16),
                pltpu.VMEM((2 * tokens, STATE), F32),
                pltpu.VMEM((tokens, STATE), BF16),
                pltpu.VMEM((chunks, STATE, CHUNK), BF16),
                pltpu.VMEM((tokens, width), BF16),
                pltpu.VMEM((chunks, width, CHUNK), BF16),
                pltpu.VMEM((tokens, width), BF16),
                pltpu.VMEM((tokens, width), F32),
                pltpu.VMEM((HEADS, tokens), F32),
                pltpu.VMEM((n_levels, HEADS, tokens), F32),
                pltpu.VMEM((chunks, 8, CHUNK), F32),
                pltpu.VMEM((chunks, HEADS, CHUNK), F32),
                pltpu.VMEM((chunks, HEADS, CHUNK), F32),
                pltpu.VMEM((chunks, HEADS, CHUNK), F32),
                pltpu.VMEM((chunks, width, CHUNK), F32),
                pltpu.VMEM((local_levels, width, STATE), F32),
                pltpu.VMEM((width, STATE), F32),
                pltpu.VMEM((width, STATE), F32),
                pltpu.VMEM((8, CHUNK), F32),
                pltpu.VMEM((n_seq, 8, CHUNK), F32),
                pltpu.VMEM((PAIRS, DIM, STATE), BF16),
                pltpu.VMEM((PAIRS, n_z, DIM, STATE), BF16),
                pltpu.VMEM((n_z, 8, CHUNK), F32),
                pltpu.VMEM((PAIRS, far_levels - 1, DIM, STATE), BF16),
                pltpu.VMEM((PAIRS, far_levels - 1, DIM, STATE), BF16),
                pltpu.VMEM((PAIRS, far_levels, 2 * DIM, STATE), BF16),
                pltpu.VMEM((PAIRS, tokens, CHUNK), BF16),
                pltpu.VMEM((rows, n_head * width), BF16),
                dma((5 + SECTIONS,)),
                dma((2 + 2 * PAIRS,)),
                dma((n_seq,)),
                dma((n_seq,)),
                dma((PAIRS, n_z)),
                dma((PAIRS, n_z)),
                dma((PAIRS, n_head)),
                dma((PAIRS, n_head)),
            ],
            compiler_params=pltpu.CompilerParams(collective_id=0, has_side_effects=True),
        )(
            b_keys.reshape(tokens, groups // 2, 2, STATE),
            c_queries.reshape(tokens, groups // 2, 2, STATE),
            values,
            gate_z,
            log_decay.T,
            level_weight.transpose(2, 1, 0),
            doc_start,
        )
        return (whole * norm_gain[None, :]).astype(BF16)

    in_specs = (
        P("seq", "head"),
        P("seq", "head"),
        P("seq", None, None),
        P("seq", None, None),
        P("seq", "head"),
        P("seq", "head", None),
        P(),
        P(),
    )
    out_specs = P(("seq", "head"), None)
    return jax.shard_map(body, mesh=mesh, in_specs=in_specs, out_specs=out_specs, check_vma=False)
```

```python
import jax
import jax.numpy as jnp
from jax import lax
from jax.experimental import pallas as pl
from jax.experimental.pallas import tpu as pltpu
from jax.sharding import PartitionSpec as P

MESH = pl.DeviceIdType.MESH
F32 = jnp.float32
BF16 = jnp.bfloat16
CHUNK = 128
SPAN = 64
HEADS = 4
DIM = 64
STATE = 128
PER_GROUP = 16
PAIRS = HEADS // 2
RESET = 128.0


def dot(a, b):
    return jnp.dot(a, b, preferred_element_type=F32)


def kernel(
    n_seq, n_head, b_hbm, c_hbm, v_hbm, g_hbm, decay_hbm, level_hbm, gain_hbm, doc_ref, out_ref,
    pair, wide, keys, query_t, raw, value_t, gate, silu, decay, level, gain,
    ds, tot, key_w, query_w, near, acc, own_state, sib_state, own_decay, all_decay,
    chip_state, chip_states, coef, own_levels, sib_levels, levels, outgoing, arrived,
    load_sem, swap_sem, decay_send, decay_recv, chip_send, chip_recv, rows_send, rows_recv,
):
    me = lax.axis_index("head")
    seq = lax.axis_index("seq")
    z, core = seq // 2, lax.rem(seq, 2)
    n_z = n_seq // 2
    far_levels = n_z.bit_length()
    group = me * HEADS // PER_GROUP
    tokens = v_hbm.shape[0]
    chunks = tokens // CHUNK
    width = HEADS * DIM
    rows_out = tokens // n_head

    loads = [
        pltpu.make_async_copy(decay_hbm, decay, load_sem.at[0]),
        pltpu.make_async_copy(v_hbm, raw, load_sem.at[1]),
        pltpu.make_async_copy(b_hbm.at[:, group // 2], pair.at[0], load_sem.at[2]),
        pltpu.make_async_copy(c_hbm.at[:, group // 2], pair.at[1], load_sem.at[3]),
        pltpu.make_async_copy(level_hbm, level, load_sem.at[4]),
        pltpu.make_async_copy(g_hbm, gate, load_sem.at[5]),
        pltpu.make_async_copy(gain_hbm, gain, load_sem.at[6]),
    ]
    for load in loads:
        load.start()

    barrier = pltpu.get_barrier_semaphore()

    def greet_head(r, _):
        pl.semaphore_signal(
            barrier, inc=1, device_id={"head": lax.rem(me + r, n_head)}, device_id_type=MESH
        )
        return 0

    def greet_seq(r, _):
        pl.semaphore_signal(
            barrier, inc=1, device_id={"seq": lax.rem(seq + r, n_seq)}, device_id_type=MESH
        )
        return 0

    lax.fori_loop(1, n_seq, greet_seq, 0)
    lax.fori_loop(1, n_head, greet_head, 0)

    loads[0].wait()
    lane4 = lax.broadcasted_iota(jnp.int32, (HEADS, CHUNK), 1)
    pieces = []
    for i in range(chunks):
        piece = decay[:, i * CHUNK : (i + 1) * CHUNK]
        for half in range(2):
            begins = doc_ref[seq * (tokens // SPAN) + 2 * i + half] != 0
            drop = jnp.where(begins, RESET, 0.0)
            piece = piece - jnp.where(lane4 == half * SPAN, drop, 0.0)
        pieces.append(piece)
    run = jnp.concatenate(pieces, axis=0)
    lane = lax.broadcasted_iota(jnp.int32, run.shape, 1)
    shift = 1
    while shift < CHUNK:
        run = run + jnp.where(lane >= shift, pltpu.roll(run, shift, 1), 0.0)
        shift *= 2
    total = jnp.broadcast_to(run[:, CHUNK - 1 : CHUNK], run.shape)
    ds[...] = jnp.zeros_like(ds)
    before = jnp.zeros((HEADS, CHUNK), F32)
    after = jnp.zeros((HEADS, CHUNK), F32)
    for i in range(chunks):
        part = slice(i * HEADS, (i + 1) * HEADS)
        ds[i, 0:HEADS, :] = run[part]
        tot[i] = total[part]
        query_w[i] = jnp.exp(before + run[part])
        before = before + total[part]
    for i in reversed(range(chunks)):
        part = slice(i * HEADS, (i + 1) * HEADS)
        key_w[i] = jnp.exp(after + (total[part] - run[part]))
        after = after + total[part]
    own_decay[...] = jnp.zeros_like(own_decay)
    own_decay[0:HEADS, :] = before

    def scaled(i, weights):
        parts = [
            value_t[i, h * DIM : (h + 1) * DIM, :].astype(F32) * weights[h : h + 1, :]
            for h in range(HEADS)
        ]
        return jnp.concatenate(parts, axis=0).astype(BF16)

    def at(i):
        return pl.ds(pl.multiple_of(i * CHUNK, CHUNK), CHUNK)

    loads[2].wait()
    wide[...] = pair[0].reshape(2 * tokens, STATE).astype(F32)
    keys[...] = wide[pl.ds(lax.rem(group, 2), tokens, stride=2), :].astype(BF16)
    loads[1].wait()
    own_state[...] = jnp.zeros_like(own_state)

    def state_step(i, _):
        value_t[i] = raw[at(i), :].T
        own_state[...] += dot(scaled(i, key_w[i]), keys[at(i), :])
        return 0

    lax.fori_loop(0, chunks, state_step, 0)

    pl.semaphore_wait(barrier, n_seq - 1 + n_head - 1)

    swap = pltpu.make_async_remote_copy(
        src_ref=own_state, dst_ref=sib_state, send_sem=swap_sem.at[0], recv_sem=swap_sem.at[1],
        device_id={"seq": 2 * z + 1 - core}, device_id_type=MESH,
    )
    swap.start()

    def decay_copy(other, slot):
        return pltpu.make_async_remote_copy(
            src_ref=own_decay, dst_ref=all_decay.at[slot], send_sem=decay_send.at[other],
            recv_sem=decay_recv.at[slot], device_id={"seq": other}, device_id_type=MESH,
        )

    def send_decay(r, _):
        decay_copy(lax.rem(seq + r, n_seq), seq).start()
        return 0

    lax.fori_loop(1, n_seq, send_decay, 0)
    all_decay[pl.ds(seq, 1)] = own_decay[...][None]

    loads[3].wait()
    wide[...] = pair[1].reshape(2 * tokens, STATE).astype(F32)

    def turn_queries(i, _):
        start = lax.rem(group, 2) + i * (2 * CHUNK)
        query_t[i] = wide[pl.ds(start, CHUNK, stride=2), :].T.astype(BF16)
        return 0

    lax.fori_loop(0, chunks, turn_queries, 0)

    sibling = 2 * z + 1 - core
    decay_copy(sibling, sibling).wait_recv()
    swap.wait_recv()

    is_upper = core == 1
    upper_decay = all_decay[2 * z + 1]
    through = jnp.exp(upper_decay)
    mine = pl.ds(pl.multiple_of(core * DIM, DIM), DIM)
    theirs = pl.ds(pl.multiple_of((1 - core) * DIM, DIM), DIM)
    for p in range(PAIRS):
        rows = pl.ds(pl.multiple_of(p * 2 * DIM + core * DIM, DIM), DIM)
        fade = jnp.where(is_upper, through[2 * p + 1 : 2 * p + 2, :], through[2 * p : 2 * p + 1, :])
        here, there = own_state[rows, :], sib_state[rows, :]
        low = jnp.where(is_upper, there, here)
        high = jnp.where(is_upper, here, there)
        chip_state[p] = (low * fade + high).astype(BF16)

    def chip_copy(p, other, slot):
        return pltpu.make_async_remote_copy(
            src_ref=chip_state.at[p], dst_ref=chip_states.at[p, slot],
            send_sem=chip_send.at[p, other], recv_sem=chip_recv.at[p, slot],
            device_id={"seq": 2 * other + core}, device_id_type=MESH,
        )

    def send_chips(p):
        def send_chip(r, _):
            chip_copy(p, lax.rem(z + r, n_z), z).start()
            return 0

        lax.fori_loop(1, n_z, send_chip, 0)

    send_chips(0)
    for p in range(PAIRS):
        rows = slice(p * 2 * DIM, (p + 1) * 2 * DIM)
        levels[p, 0] = jnp.where(is_upper, sib_state[rows, :], 0.0).astype(BF16)

    loads[4].wait()
    loads[5].wait()
    acc[...] = jnp.zeros_like(acc)
    sub_i = lax.broadcasted_iota(jnp.int32, (CHUNK, CHUNK), 0)
    lane_i = lax.broadcasted_iota(jnp.int32, (CHUNK, CHUNK), 1)
    causal = sub_i <= lane_i
    early = sub_i < SPAN
    first_half = lax.broadcasted_iota(jnp.int32, (1, CHUNK), 1) < SPAN
    local_levels = acc.shape[0]

    def near_step(i, _):
        g = gate[at(i), :].astype(F32)
        silu[at(i), :] = g / (1.0 + jnp.exp(-g))
        turned = query_t[i]
        block = keys[at(i), :]
        scores = dot(block, turned)
        run_i = ds[i]
        columns = run_i.T
        weight = jnp.exp(run_i)
        tot_i = tot[i]
        into = dot(
            acc[...].reshape(local_levels * width, STATE).astype(BF16), turned
        ).reshape(local_levels, width, CHUNK)
        for h in range(HEADS):
            rows = slice(h * DIM, (h + 1) * DIM)
            fall = run_i[h : h + 1, :] - jnp.broadcast_to(columns[:, h : h + 1], (CHUNK, CHUNK))
            same = level[0, h : h + 1, at(i)]
            cross = jnp.where(first_half, same, level[1, h : h + 1, at(i)])
            mixed = jnp.exp(jnp.where(causal, fall, -1e30)) * jnp.where(early, cross, same) * scores
            result = dot(value_t[i, rows, :], mixed.astype(BF16))
            for k in range(local_levels):
                on = (lax.shift_right_logical(i, k) & 1).astype(F32)
                factor = level[2 + k, h : h + 1, at(i)] * weight[h : h + 1, :] * on
                result = result + into[k, rows, :] * factor
            near[i, rows, :] = result
        state = dot(scaled(i, jnp.exp(tot_i - run_i[0:HEADS])), block)
        keep = jnp.exp(tot_i)
        for k in range(local_levels):
            low = (1 - (lax.shift_right_logical(i, k) & 1)).astype(F32)
            held = (lax.rem(i, 2 ** (k + 1)) != 0).astype(F32)
            for h in range(HEADS):
                rows = slice(h * DIM, (h + 1) * DIM)
                acc[k, rows, :] = acc[k, rows, :] * (keep[h : h + 1, :] * held) + state[rows, :] * low
        return 0

    lax.fori_loop(0, chunks, near_step, 0)
    for p in range(1, PAIRS):
        send_chips(p)

    def wait_decay(r, _):
        other = lax.rem(seq + r, n_seq)

        @pl.when(other != sibling)
        def _():
            decay_copy(other, other).wait_recv()

        return 0

    lax.fori_loop(1, n_seq, wait_decay, 0)
    gap = jnp.zeros((8, CHUNK), F32)
    for j in reversed(range(n_z)):
        coef[j] = jnp.where(j < z, jnp.exp(gap), 0.0)
        gap = gap + jnp.where(j < z, all_decay[2 * j] + all_decay[2 * j + 1], 0.0)

    def row_copy(p, target, source):
        return pltpu.make_async_remote_copy(
            src_ref=outgoing.at[p, pl.ds(pl.multiple_of(target * rows_out, rows_out), rows_out), :],
            dst_ref=arrived.at[:, pl.ds(pl.multiple_of(source * width + p * CHUNK, CHUNK), CHUNK)],
            send_sem=rows_send.at[p, target], recv_sem=rows_recv.at[p, source],
            device_id={"head": target}, device_id_type=MESH,
        )

    wide_chunk = 2 * CHUNK
    per_chunk = wide_chunk // rows_out
    own_chunk = me // per_chunk
    base = level.shape[0] - far_levels
    shares = []
    beyond = jnp.where(is_upper, jnp.exp(all_decay[2 * z])[0:HEADS], 1.0)

    for p in range(PAIRS):
        def wait_chip(r, _):
            other = lax.rem(z + r, n_z)
            chip_copy(p, other, other).wait_recv()
            return 0

        lax.fori_loop(1, n_z, wait_chip, 0)
        for k in range(far_levels - 1):
            first = (lax.shift_right_logical(z, k) ^ 1) * 2**k
            sums = jnp.zeros((DIM, STATE), F32)
            for n in range(2**k):
                row = coef[first + n]
                fade = jnp.where(is_upper, row[2 * p + 1 : 2 * p + 2, :], row[2 * p : 2 * p + 1, :])
                sums = sums + chip_states[p, first + n].astype(F32) * fade
            own_levels[p, k] = sums.astype(BF16)
        share = pltpu.make_async_remote_copy(
            src_ref=own_levels.at[p], dst_ref=sib_levels.at[p], send_sem=swap_sem.at[2 + 2 * p],
            recv_sem=swap_sem.at[3 + 2 * p], device_id={"seq": 2 * z + 1 - core},
            device_id_type=MESH,
        )
        share.start()
        shares.append(share)
        for k in range(far_levels - 1):
            levels[p, 1 + k, mine, :] = own_levels[p, k]
        share.wait_recv()
        for k in range(far_levels - 1):
            levels[p, 1 + k, theirs, :] = sib_levels[p, k]

        def far_step(r, _):
            i = lax.rem(own_chunk + r, chunks // 2)
            tokens_i = pl.ds(pl.multiple_of(i * wide_chunk, wide_chunk), wide_chunk)
            queries = jnp.concatenate([query_t[2 * i], query_t[2 * i + 1]], axis=1)
            into = dot(
                levels[p].reshape(far_levels * 2 * DIM, STATE), queries
            ).reshape(far_levels, 2 * DIM, wide_chunk)
            weights = [query_w[2 * i], query_w[2 * i + 1]]
            weight = jnp.concatenate(weights, axis=1)
            further = jnp.concatenate([w * beyond for w in weights], axis=1)
            columns = []
            for j in range(2):
                h = 2 * p + j
                rows = slice(h * DIM, (h + 1) * DIM)
                result = jnp.concatenate([near[2 * i, rows, :], near[2 * i + 1, rows, :]], axis=1)
                for k in range(far_levels):
                    from_start = weight if k == 0 else further
                    factor = level[base + k, h : h + 1, tokens_i] * from_start[h : h + 1, :]
                    result = result + into[k, j * DIM : (j + 1) * DIM, :] * factor
                columns.append(result)
            mixed = jnp.concatenate(columns, axis=0).T
            gates = silu[tokens_i, p * CHUNK : (p + 1) * CHUNK]
            outgoing[p, tokens_i, :] = (mixed * gates).astype(BF16)

            def send_rows(k, _):
                target = i * per_chunk + lax.rem(me + k, per_chunk)

                @pl.when(target != me)
                def _():
                    row_copy(p, target, me).start()

                return 0

            lax.fori_loop(0, per_chunk, send_rows, 0)
            return 0

        lax.fori_loop(0, chunks // 2, far_step, 0)
        arrived[:, pl.ds(pl.multiple_of(me * width + p * CHUNK, CHUNK), CHUNK)] = outgoing[
            p, pl.ds(pl.multiple_of(me * rows_out, rows_out), rows_out), :
        ]

    loads[6].wait()
    group_width = PER_GROUP * DIM
    per_group = group_width // width
    groups = n_head // per_group

    def norm_step(r, _):
        g = lax.rem(me // per_group - r + groups, groups)
        for k in range(per_group):
            source = g * per_group + k

            @pl.when(source != me)
            def _():
                for p in range(PAIRS):
                    row_copy(p, source, source).wait_recv()

        x = arrived[:, pl.ds(pl.multiple_of(g * group_width, group_width), group_width)].astype(F32)
        inverse = lax.rsqrt(jnp.sum(x * x, axis=1, keepdims=True) * (1.0 / group_width) + 1e-05)
        for k in range(group_width // CHUNK):
            y = x[:, k * CHUNK : (k + 1) * CHUNK] * inverse * gain[pl.ds(g * (group_width // CHUNK) + k, 1), :]
            out_ref[:, pl.ds(pl.multiple_of(g * group_width + k * CHUNK, CHUNK), CHUNK)] = y.astype(BF16)
        return 0

    lax.fori_loop(0, groups, norm_step, 0)

    def drain_rows(r, _):
        for p in range(PAIRS):
            row_copy(p, lax.rem(me + r, n_head), me).wait_send()
        return 0

    lax.fori_loop(1, n_head, drain_rows, 0)

    def drain_decay(r, _):
        decay_copy(lax.rem(seq + r, n_seq), seq).wait_send()
        return 0

    lax.fori_loop(1, n_seq, drain_decay, 0)

    def drain_chip(r, _):
        for p in range(PAIRS):
            chip_copy(p, lax.rem(z + r, n_z), z).wait_send()
        return 0

    lax.fori_loop(1, n_z, drain_chip, 0)
    swap.wait_send()
    for share in shares:
        share.wait_send()


def solution(mesh):
    n_seq, n_head = mesh.shape["seq"], mesh.shape["head"]
    n_z = n_seq // 2

    def body(values, gate_z, b_keys, c_queries, log_decay, level_weight, doc_start, norm_gain):
        tokens, width = values.shape
        chunks = tokens // CHUNK
        n_levels = level_weight.shape[2]
        far_levels = n_z.bit_length()
        local_levels = chunks.bit_length() - 1
        groups = b_keys.shape[1]
        any_space = pl.BlockSpec(memory_space=pl.ANY)
        rows = tokens // n_head
        dma = pltpu.SemaphoreType.DMA

        def run(*args):
            return kernel(n_seq, n_head, *args)

        return pl.pallas_call(
            run,
            out_shape=jax.ShapeDtypeStruct((rows, n_head * width), BF16),
            in_specs=[any_space] * 7 + [pl.BlockSpec(memory_space=pltpu.SMEM)],
            out_specs=pl.BlockSpec(memory_space=pltpu.VMEM),
            scratch_shapes=[
                pltpu.VMEM((2, tokens, 2, STATE), BF16),
                pltpu.VMEM((2 * tokens, STATE), F32),
                pltpu.VMEM((tokens, STATE), BF16),
                pltpu.VMEM((chunks, STATE, CHUNK), BF16),
                pltpu.VMEM((tokens, width), BF16),
                pltpu.VMEM((chunks, width, CHUNK), BF16),
                pltpu.VMEM((tokens, width), BF16),
                pltpu.VMEM((tokens, width), F32),
                pltpu.VMEM((HEADS, tokens), F32),
                pltpu.VMEM((n_levels, HEADS, tokens), F32),
                pltpu.VMEM((n_head * width // CHUNK, CHUNK), F32),
                pltpu.VMEM((chunks, 8, CHUNK), F32),
                pltpu.VMEM((chunks, HEADS, CHUNK), F32),
                pltpu.VMEM((chunks, HEADS, CHUNK), F32),
                pltpu.VMEM((chunks, HEADS, CHUNK), F32),
                pltpu.VMEM((chunks, width, CHUNK), F32),
                pltpu.VMEM((local_levels, width, STATE), F32),
                pltpu.VMEM((width, STATE), F32),
                pltpu.VMEM((width, STATE), F32),
                pltpu.VMEM((8, CHUNK), F32),
                pltpu.VMEM((n_seq, 8, CHUNK), F32),
                pltpu.VMEM((PAIRS, DIM, STATE), BF16),
                pltpu.VMEM((PAIRS, n_z, DIM, STATE), BF16),
                pltpu.VMEM((n_z, 8, CHUNK), F32),
                pltpu.VMEM((PAIRS, far_levels - 1, DIM, STATE), BF16),
                pltpu.VMEM((PAIRS, far_levels - 1, DIM, STATE), BF16),
                pltpu.VMEM((PAIRS, far_levels, 2 * DIM, STATE), BF16),
                pltpu.VMEM((PAIRS, tokens, CHUNK), BF16),
                pltpu.VMEM((rows, n_head * width), BF16),
                dma((7,)),
                dma((2 + 2 * PAIRS,)),
                dma((n_seq,)),
                dma((n_seq,)),
                dma((PAIRS, n_z)),
                dma((PAIRS, n_z)),
                dma((PAIRS, n_head)),
                dma((PAIRS, n_head)),
            ],
            compiler_params=pltpu.CompilerParams(collective_id=0, has_side_effects=True, vmem_limit_bytes=54200 * 1024),
        )(
            b_keys.reshape(tokens, groups // 2, 2, STATE),
            c_queries.reshape(tokens, groups // 2, 2, STATE),
            values,
            gate_z,
            log_decay.T,
            level_weight.transpose(2, 1, 0),
            norm_gain.reshape(n_head * width // CHUNK, CHUNK),
            doc_start,
        )

    in_specs = (
        P("seq", "head"),
        P("seq", "head"),
        P("seq", None, None),
        P("seq", None, None),
        P("seq", "head"),
        P("seq", "head", None),
        P(),
        P(),
    )
    out_specs = P(("seq", "head"), None)
    return jax.shard_map(body, mesh=mesh, in_specs=in_specs, out_specs=out_specs, check_vma=False)
```
